32 devices in a mesh: gx: 8 (over z, x), gy: 2 (over y), gz: 2 (over core).
Axes of the slice: x: 2, y: 2, z: 4, core: 2. Of those that a mesh axis runs over, the one named last changes fastest.
Arguments:
- velocity: float32 [3, 128, 64, 256], P(None, 'gx', 'gy', 'gz'), may hold values from -6 to 6
- conv_prev: float32 [3, 128, 64, 256], P(None, 'gx', 'gy', 'gz'), may hold values from -8 to 8
Outputs:
- convection: float32 [3, 128, 64, 256], P(None, 'gx', 'gy', 'gz')
- updated: float32 [3, 128, 64, 256], P(None, 'gx', 'gy', 'gz')
The draws below stay inside these ranges and needn't reach their ends.
All inputs are finite; a program needn't handle non-finite values.
Results may differ from the reference program's by a relative error of at most 0.00011.
Values sent between devices are 32-bit elements; how exact they have to be, the bound alone decides.
A program may use at most 64 MiB of HBM per device.

```python
import jax
import jax.numpy as jnp
from jax import lax

CY = 32
NX = 128
NY = 64
NZ = 256


def draw_velocity(key, part):
    noise_key, factor_key = jax.random.split(key)
    shape = (3, NX, NY, NZ)
    factor = jnp.exp(jax.random.uniform(factor_key, shape, jnp.float32, -0.5, 0.5))
    values = jax.random.truncated_normal(noise_key, -4.0, 4.0, shape, jnp.float32) * factor
    return jnp.clip(values, -6.0, 6.0)


def block_scale(rng, shape, cuts, least, largest):
    level, own = 1.0, jax.random.fold_in(rng, 6)
    for position, shards_of in cuts:
        heights = jnp.exp(jax.random.uniform(jax.random.fold_in(own, position), (shards_of,), jnp.float32, least / len(cuts), largest / len(cuts)))
        level = level * jnp.repeat(heights, shape[position] // shards_of).reshape([-1 if axis == position else 1 for axis in range(len(shape))])
    return level


def bell_draw(stream_key, extent, scale, most, shards=(), held_as=jnp.bfloat16):
    array = scale * jax.random.normal(stream_key, extent, jnp.float32)
    if shards:
        array = array * block_scale(stream_key, extent, shards, -0.22, 0.18)
    return jnp.clip(array, -most, most).astype(held_as)


def setup_inputs(seed: int = 0) -> dict:
    key_list = jax.random.split(jax.random.key(seed), 3)
    return {
        "velocity": draw_velocity(jax.random.fold_in(key_list[2], 71), 0),
        "conv_prev": bell_draw(key_list[1], (3, NX, NY, NZ), 2.0, 8.0, ((1, 8), (2, 2), (3, 2)), jnp.float32),
    }


time_step = 1.0
gamma_now = 5.0 / 12.0
zeta_old = -17.0 / 60.0
viscosity = 0.1


def line_table(off_value, center, total):
    def advance(previous, unused):
        pivot = center - off_value * previous
        ratio = off_value / pivot
        return ratio, (ratio, pivot)

    _, (ratios, pivots) = lax.scan(advance, jnp.zeros((), jnp.float32), None, length=total)
    return ratios, pivots


def thomas(values, off_value, center, axis):
    moved = jnp.moveaxis(values, axis, 0)
    ratios, pivots = line_table(off_value, center, moved.shape[0])

    def forward(carry, items):
        value, ratio, pivot = items
        fresh = value / pivot - ratio * carry
        return fresh, fresh

    _, reduced = lax.scan(forward, jnp.zeros(moved.shape[1:], jnp.float32), (moved, ratios, pivots))

    def backward(carry, items):
        value, ratio = items
        fresh = value - ratio * carry
        return fresh, fresh

    _, solved = lax.scan(backward, jnp.zeros(moved.shape[1:], jnp.float32), (reduced, ratios), reverse=True)
    return jnp.moveaxis(solved, 0, axis)


def compact_sides(field, axis):
    total = field.shape[axis]
    widths = [(0, 0), (0, 0), (0, 0)]
    widths[axis] = (2, 2)
    padded = jnp.pad(field, widths)

    def shifted(shift):
        return lax.slice_in_dim(padded, 2 + shift, 2 + shift + total, axis=axis)

    centre = shifted(0)
    first = (7.0 / 9.0) * (shifted(1) - shifted(-1)) + (1.0 / 36.0) * (shifted(2) - shifted(-2))
    second = (12.0 / 11.0) * (shifted(1) - 2.0 * centre + shifted(-1)) + (3.0 / 44.0) * (shifted(2) - 2.0 * centre + shifted(-2))
    return first, second


def span_terms(field):
    def shifted(shift):
        return jnp.roll(field, -shift, axis=2)

    first = (45.0 * (shifted(1) - shifted(-1)) - 9.0 * (shifted(2) - shifted(-2)) + (shifted(3) - shifted(-3))) / 60.0
    second = (2.0 * (shifted(3) + shifted(-3)) - 27.0 * (shifted(2) + shifted(-2)) + 270.0 * (shifted(1) + shifted(-1)) - 490.0 * field) / 180.0
    return first, second


def reference(velocity, conv_prev):
    beta = 4.0 * CY * CY

    def component(index):
        field = velocity[index]
        rhs_first, rhs_second = compact_sides(field, 0)
        first_x = thomas(rhs_first, 1.0 / 3.0, 1.0, 0)
        second_x = thomas(rhs_second, 2.0 / 11.0, 1.0, 0)
        rhs_first, rhs_second = compact_sides(field, 1)
        first_y = thomas(rhs_first, 1.0 / 3.0, 1.0, 1)
        second_y = thomas(rhs_second, 2.0 / 11.0, 1.0, 1)
        first_z, second_z = span_terms(field)
        convection = velocity[0] * first_x + velocity[1] * first_y + velocity[2] * first_z
        explicit = field - time_step * (gamma_now * convection + zeta_old * conv_prev[index]) + viscosity * (second_x + second_y + second_z)
        updated = thomas(explicit, -beta, 1.0 + 2.0 * beta, 1)
        return convection, updated

    convection, updated = lax.map(component, jnp.arange(3))
    return convection, updated
```

```python
import collections
import functools

import jax
import jax.numpy as jnp
import numpy as np
from jax import lax
from jax.experimental import pallas as pl
from jax.experimental.pallas import tpu as pltpu
from jax.sharding import PartitionSpec as P

MESH = pl.DeviceIdType.MESH
WIDE = 8
time_step = 1.0
gamma_now = 5.0 / 12.0
zeta_old = -17.0 / 60.0
viscosity = 0.1

FIRST = {1: 7.0 / 9.0, -1: -7.0 / 9.0, 2: 1.0 / 36.0, -2: -1.0 / 36.0}
SECOND = {1: 12.0 / 11.0, -1: 12.0 / 11.0, 2: 3.0 / 44.0, -2: 3.0 / 44.0, 0: -24.0 / 11.0 - 6.0 / 44.0}
COMPACT = ((1.0 / 3.0, 1.0, FIRST), (2.0 / 11.0, 1.0, SECOND))


class System:
    def __init__(self, off, mid, stencil, count, m):
        n = count * m
        rho = np.zeros(n + 2)
        last = 0.0
        for j in range(n + 2):
            last = -off / (mid + off * last)
            rho[j] = last

        def u(j, ref):
            if j < 0:
                return 0.0
            if j <= ref:
                return float(np.prod(rho[j:ref]))
            return 1.0 / float(np.prod(rho[ref:j]))

        def v(j, ref):
            return u(n - 1 - j, n - 1 - ref)

        def inv(i, j):
            low = rho[i - 1] if i > 0 else 0.0
            high = rho[n - 2 - i] if i < n - 1 else 0.0
            diag = 1.0 / (mid + off * low + off * high)
            return diag * (u(j, i) if j <= i else v(j, i))

        def b(j, col):
            return stencil.get(col - j, 0.0)

        self.off, self.m, self.count = off, m, count
        self.right, self.left = np.zeros((count, m)), np.zeros((count, m))
        self.fix_low, self.fix_high = np.zeros((count, 3)), np.zeros((count, 3))
        self.d = np.zeros((count, 4))
        self.t = np.zeros((count, 2))
        self.weights = np.zeros((2, count, 2, count))
        for p in range(count):
            start, end = p * m, p * m + m - 1
            for k in range(m):
                col = start + k
                rows = [j for j in range(col - 2, col + 3) if 0 <= j < n]
                self.right[p, k] = sum(u(j, end) * b(j, col) for j in rows)
                self.left[p, k] = sum(v(j, start) * b(j, col) for j in rows)
            if p > 0:
                e = start - 1
                self.fix_low[p] = (
                    sum((inv(e, j) - inv(e, e) * u(j, e)) * b(j, e) for j in (e + 1, e + 2)),
                    (inv(e, e + 1) - inv(e, e) * u(e + 1, e)) * b(e + 1, e - 1),
                    (inv(e, e - 1) - inv(e, e + 1) * v(e - 1, e + 1)) * b(e - 1, e + 1),
                )
                self.d[p, 0], self.d[p, 1] = inv(e, e), inv(e, e + 1)
                self.t[p, 0] = u(e, end)
                for q in range(count):
                    if q < p:
                        self.weights[0, q, 0, p] = inv(e, q * m + m - 1)
                    else:
                        self.weights[0, q, 1, p] = inv(e, q * m)
            if p < count - 1:
                f = end + 1
                self.fix_high[p] = (
                    sum((inv(f, j) - inv(f, f) * v(j, f)) * b(j, f) for j in (f - 1, f - 2)),
                    (inv(f, f - 1) - inv(f, f) * v(f - 1, f)) * b(f - 1, f + 1),
                    (inv(f, f + 1) - inv(f, f - 1) * u(f + 1, f - 1)) * b(f + 1, f - 1),
                )
                self.d[p, 2], self.d[p, 3] = inv(f, f - 1), inv(f, f)
                self.t[p, 1] = v(f, start)
                for q in range(count):
                    if q > p:
                        self.weights[1, q, 1, p] = inv(f, q * m)
                    else:
                        self.weights[1, q, 0, p] = inv(f, q * m + m - 1)
        pivots, ratios, last = [], [], 0.0
        for _ in range(m):
            pivot = mid - off * last
            last = off / pivot
            pivots.append(pivot)
            ratios.append(last)
        self.scale = [float(1.0 / pivot) for pivot in pivots]
        self.ratio = [float(ratio) for ratio in ratios]
        unit = np.zeros(m)
        unit[0] = 1.0
        self.low = [-off * value for value in self.solve(list(unit))]
        self.high = self.low[::-1]

    def solve(self, rows):
        done, carry = [], None
        for i, row in enumerate(rows):
            fresh = row * self.scale[i]
            carry = fresh if carry is None else fresh - self.ratio[i] * carry
            done.append(carry)
        for i in range(self.m - 2, -1, -1):
            done[i] = done[i] - self.ratio[i] * done[i + 1]
        return done


def pick(place, values):
    values = [float(np.float32(value)) for value in values]
    common = collections.Counter(values).most_common(1)[0][0]
    result = jnp.float32(common)
    for index, value in enumerate(values):
        if value != common:
            result = jnp.where(place == index, jnp.float32(value), result)
    return result


def sides(at):
    odd_1, even_1 = at(1) - at(-1), at(1) + at(-1)
    odd_2, even_2 = at(2) - at(-2), at(2) + at(-2)
    first = FIRST[1] * odd_1 + FIRST[2] * odd_2
    second = SECOND[1] * even_1 + (SECOND[2] * even_2 + SECOND[0] * at(0))
    return first, second


def total(terms):
    return functools.reduce(lambda a, b: a + b, terms)


def kernel(
    cfg, v_hbm, cp_hbm, conv, base, ends_w, shape_w,
    v, cp, zo, xlo, xhi, gx, gr, to, st, ti, yout, yin, vt, fy, sy, expl, et, gw, gwr, tally,
    load, r1, r2, yr, zr, wr, hs, hr, sent,
):
    nc, mx, my, nz, px, py, size, groups = cfg
    rows = 2 * my // size
    me = lax.axis_index("gx")
    wall = lax.axis_index("gy")
    core = lax.axis_index("gz")
    group, rank = me // size, lax.rem(me, size)
    sys_x = [System(*pair, px, mx) for pair in COMPACT]
    sys_y = [System(*pair, py, my) for pair in COMPACT]
    beta = 4.0 * my * my
    sys_w = System(-beta, 1.0 + 2.0 * beta, {0: 1.0}, py, my)

    barrier = pltpu.get_barrier_semaphore()
    for d in range(1, px):
        pl.semaphore_signal(barrier, inc=1, device_id={"gx": lax.rem(me + d, px)}, device_id_type=MESH)
    for d in range(1, py):
        pl.semaphore_signal(barrier, inc=1, device_id={"gy": lax.rem(wall + d, py)}, device_id_type=MESH)
    pl.semaphore_signal(barrier, inc=1, device_id={"gz": 1 - core}, device_id_type=MESH)

    reads = [pltpu.make_async_copy(v_hbm.at[c], v.at[c], load.at[c]) for c in range(nc)]
    reads.append(pltpu.make_async_copy(cp_hbm, cp, load.at[nc]))
    for read in reads:
        read.start()

    def remote(src, dst, send, recv, **target):
        return pltpu.make_async_remote_copy(
            src_ref=src, dst_ref=dst, send_sem=send, recv_sem=recv,
            device_id=target, device_id_type=MESH,
        )

    def arrived(ref, sem):
        pltpu.make_async_copy(ref, ref, sem).wait()

    def other(d):
        if size & (size - 1):
            return lax.rem(rank + d, size)
        result, bit = 0, 1
        while bit < size:
            mine = lax.rem(rank // bit, 2)
            result = result + bit * ((1 - mine) if d & bit else mine)
            bit *= 2
        return result

    weigh_x = [
        [[pick(me, table[:, i]) for i in range(mx)] for table in (s.right, s.left)] for s in sys_x
    ]

    def sums_x(c):
        def step(b, _):
            part = [v[c, pl.ds(pl.multiple_of(i * my + b * 8, 8), 8), :] for i in range(mx)]
            for s in range(2):
                for way in range(2):
                    value = total([weigh_x[s][way][i] * part[i] for i in range(mx)])
                    flat = s * my + b * 8
                    owner = flat // rows
                    at = owner * 2 * rows + way * rows + lax.rem(flat, rows)
                    gx[c, pl.ds(pl.multiple_of(at, 8), 8), :] = value
            return 0

        lax.fori_loop(0, my // 8, step, 0)

    own = pl.ds(pl.multiple_of(rank * 2 * rows, 8), 2 * rows)
    for c in range(nc):
        reads[c].wait()
        sums_x(c)
        if c == 0:
            pl.semaphore_wait(barrier, px - 1 + py - 1 + 1)
        for d in range(size - 1, 0, -1):
            t = other(d)
            remote(
                gx.at[c, pl.ds(pl.multiple_of(t * 2 * rows, 8), 2 * rows)], gr.at[c, rank],
                sent.at[0], r1.at[c], gx=group * size + t,
            ).start()
        gr[c, rank] = gx[c, own, :]
        remote(v.at[c], zo.at[c], sent.at[1], zr.at[c], gz=1 - core).start()

    up = remote(v.at[:, pl.ds((mx - 2) * my, 2 * my)], xlo, hs.at[0], hr.at[0], gx=lax.rem(me + 1, px))
    down = remote(v.at[:, pl.ds(0, 2 * my)], xhi, hs.at[1], hr.at[1], gx=lax.rem(me + px - 1, px))

    @pl.when(me < px - 1)
    def _():
        up.start()

    @pl.when(me > 0)
    def _():
        down.start()

    def yrow(ref, c, y):
        return ref[c, pl.ds(y, mx, stride=my), :]

    weigh_y = [
        [[pick(wall, table[:, i]) for i in range(my)] for table in (s.right, s.left)] for s in sys_y
    ]

    def sums_y(c, _):
        sums = [[None, None], [None, None]]
        for i in range(my):
            row = yrow(v, c, i)
            vt[c, i] = row
            if i < 2:
                yout[c, 1, i] = row
            if i >= my - 2:
                yout[c, 0, i - (my - 2)] = row
            for s in range(2):
                for way in range(2):
                    term = weigh_y[s][way][i] * row
                    sums[s][way] = term if i == 0 else sums[s][way] + term
        for s in range(2):
            for way in range(2):
                yout[c, way, 2 + s] = sums[s][way]
        for d in range(1, py):
            peer = lax.rem(wall + d, py)
            way = jnp.where(peer > wall, 0, 1)
            remote(yout.at[c, way], yin.at[c, d - 1], sent.at[0], yr.at[c], gy=peer).start()
        return 0

    for c in range(nc):
        sums_y(c, 0)

    for i in range(my):
        shape_w[0, pl.ds(i, 1), :] = jnp.full((1, nz), sys_w.low[i], jnp.float32)
        shape_w[1, pl.ds(i, 1), :] = jnp.full((1, nz), sys_w.high[i], jnp.float32)

    slab = min(128, mx * my)
    lane = lax.broadcasted_iota(jnp.int32, (slab, nz), 1)
    reads[nc].wait()

    def solve_z(c):
        def step(index, _):
            part = pl.ds(pl.multiple_of(index * slab, slab), slab)
            mine, rest = v[c, part, :], zo[c, part, :]

            def after(k):
                return pltpu.roll(jnp.where(lane < k, rest, mine), nz - k, 1)

            def before(k):
                return pltpu.roll(jnp.where(lane >= nz - k, rest, mine), k, 1)

            high, low = [after(k) for k in (1, 2, 3)], [before(k) for k in (1, 2, 3)]
            odd = [a - b for a, b in zip(high, low)]
            even = [a + b for a, b in zip(high, low)]
            first = (45.0 / 60.0) * odd[0] - (9.0 / 60.0) * odd[1] + (1.0 / 60.0) * odd[2]
            bend = (
                (viscosity * 2.0 / 180.0) * even[2] - (viscosity * 27.0 / 180.0) * even[1]
                + (viscosity * 270.0 / 180.0) * even[0] + (1.0 - viscosity * 490.0 / 180.0) * mine
            )
            conv[c, part, :] = v[2, part, :] * first
            expl[c, part, :] = bend - (time_step * zeta_old) * cp[c, part, :]
            return 0

        arrived(zo.at[c], zr.at[c])
        lax.fori_loop(0, mx * my // slab, step, 0)

    half = size // 2
    share = rank // half

    def table(field):
        return [
            pick(group * 2 + share, [field(sys_x[s], g * size + m) for g in range(groups) for s in range(2)])
            for m in range(size)
        ]

    t0, t1 = (table(lambda s, p, k=k: s.t[p, k]) for k in range(2))
    d0, d1, d2, d3 = (table(lambda s, p, k=k: s.d[p, k]) for k in range(4))

    def exchange(c):
        arrived(gr.at[c, pl.ds(0, size - 1)], r1.at[c])
        below, above = [None] * size, [None] * size
        for m in range(size):
            here = gr[c, m, pl.ds(0, rows), :]
            below[m] = here if m == 0 else here + t0[m] * below[m - 1]
        for m in reversed(range(size)):
            here = gr[c, m, pl.ds(rows, rows), :]
            above[m] = here if m == size - 1 else here + t1[m] * above[m + 1]
        if groups > 1:
            st[c, 0] = below[size - 1]
            st[c, 1] = above[0]
            for dg in range(1, groups):
                there = lax.rem(group + dg, groups)
                way = jnp.where(there > group, 0, 1)
                at = pl.multiple_of(4 * my + (dg - 1) * 2 * my + rank * rows, 8)
                for d in range(size - 1, -1, -1):
                    m = other(d)
                    remote(
                        st.at[c, way], ti.at[c, pl.ds(at, rows)], sent.at[0], r2.at[c],
                        gx=there * size + m,
                    ).start()
        for m in range(size):
            low = d1[m] * above[m]
            to[c, m, pl.ds(0, rows), :] = low if m == 0 else low + d0[m] * below[m - 1]
            high = d2[m] * below[m]
            to[c, m, pl.ds(rows, rows), :] = high if m == size - 1 else high + d3[m] * above[m + 1]
        for d in range(size - 1, 0, -1):
            t = other(d)
            remote(to.at[c, t], ti.at[c, own], sent.at[0], r2.at[c], gx=group * size + t).start()
        ti[c, own, :] = to[c, rank]

    def gathered(system, side):
        def way(q, p):
            return 1 - side if q == p else (0 if q < p else 1)

        return [
            pick(wall, [system.weights[side, (p - d) % py, way((p - d) % py, p), p] for p in range(py)])
            for d in range(py)
        ]

    low_y = [[pick(wall, -s.off * s.fix_low[:, k]) for k in range(3)] for s in sys_y]
    high_y = [[pick(wall, -s.off * s.fix_high[:, k]) for k in range(3)] for s in sys_y]
    outer_y = [[gathered(s, side) for side in range(2)] for s in sys_y]
    wide = WIDE

    def solve_y(index, _):
        c = index // (mx // wide)
        first_row = pl.multiple_of(lax.rem(index, mx // wide) * wide, wide)
        part = pl.ds(first_row, wide)
        rows_y = [jnp.where(wall > 0, yin[c, 0, k, part, :], 0.0) for k in range(2)]
        rows_y += [vt[c, y, part, :] for y in range(my)]
        rows_y += [jnp.where(wall < py - 1, yin[c, py - 2, k, part, :], 0.0) for k in range(2)]
        pairs = [sides(lambda k, i=i: rows_y[i + 2 + k]) for i in range(my)]
        for s, out in ((0, fy), (1, sy)):
            rhs = [pair[s] for pair in pairs]
            ends = [
                total(
                    [outer_y[s][side][0] * yout[c, 1 - side, 2 + s, part, :]]
                    + [outer_y[s][side][d] * yin[c, d - 1, 2 + s, part, :] for d in range(1, py)]
                )
                for side in range(2)
            ]
            rhs[0] = rhs[0] + (
                low_y[s][0] * rows_y[1] + low_y[s][1] * rows_y[0] + low_y[s][2] * rows_y[2]
                - sys_y[s].off * ends[0]
            )
            rhs[my - 1] = rhs[my - 1] + (
                high_y[s][0] * rows_y[my + 2] + high_y[s][1] * rows_y[my + 3] + high_y[s][2] * rows_y[my + 1]
                - sys_y[s].off * ends[1]
            )
            for i, value in enumerate(sys_y[s].solve(rhs)):
                out[c, pl.ds(first_row * my + i, wide, stride=my), :] = value
        return 0

    low_x = [[pick(me, -s.off * s.fix_low[:, k]) for k in range(3)] for s in sys_x]
    high_x = [[pick(me, -s.off * s.fix_high[:, k]) for k in range(3)] for s in sys_x]
    tile = 16 if my % 16 == 0 else 8

    def solve_x(index, _):
        c = index // (my // tile)
        start = pl.multiple_of(lax.rem(index, my // tile) * tile, tile)
        rows_x = [xlo[c, pl.ds(k * my + start, tile), :] for k in range(2)]
        rows_x += [v[c, pl.ds(i * my + start, tile), :] for i in range(mx)]
        rows_x += [xhi[c, pl.ds(k * my + start, tile), :] for k in range(2)]
        pairs = [sides(lambda k, i=i: rows_x[i + 2 + k]) for i in range(mx)]
        solved = []
        for s in range(2):
            rhs = [pair[s] for pair in pairs]
            rhs[0] = rhs[0] + (
                low_x[s][0] * rows_x[1] + low_x[s][1] * rows_x[0] + low_x[s][2] * rows_x[2]
            )
            rhs[mx - 1] = rhs[mx - 1] + (
                high_x[s][0] * rows_x[mx + 2] + high_x[s][1] * rows_x[mx + 3] + high_x[s][2] * rows_x[mx + 1]
            )
            solved.append(sys_x[s].solve(rhs))
        for i in range(mx):
            part = pl.ds(i * my + start, tile)
            moved = conv[c, part, :] + v[0, part, :] * solved[0][i] + v[1, part, :] * fy[c, part, :]
            conv[c, part, :] = moved
            expl[c, part, :] = (
                expl[c, part, :] - (time_step * gamma_now) * moved
                + viscosity * (solved[1][i] + sy[c, part, :])
            )
        return 0

    solve_z(0)
    for c in range(nc):
        exchange(c)
    for c in range(1, nc):
        solve_z(c)
    for c in range(nc):
        arrived(yin.at[c], yr.at[c])
    lax.fori_loop(0, nc * (mx // wide), solve_y, 0)

    @pl.when(me > 0)
    def _():
        up.wait_recv()

    @pl.when(me == 0)
    def _():
        xlo[...] = jnp.zeros_like(xlo)

    @pl.when(me < px - 1)
    def _():
        down.wait_recv()

    @pl.when(me == px - 1)
    def _():
        xhi[...] = jnp.zeros_like(xhi)

    lax.fori_loop(0, nc * (my // tile), solve_x, 0)

    def far(s, side, dg):
        values = []
        for p in range(px):
            g, q = p // size, (p // size - dg) % groups
            if q < g:
                value = s.d[p, 2 * side]
                for k in range((q + 1) * size, p + side):
                    value = value * s.t[k, 0]
            else:
                value = s.d[p, 2 * side + 1]
                for k in range(p + side, q * size):
                    value = value * s.t[k, 1]
            values.append(value)
        return pick(me, values)

    far_x = [[[far(s, side, dg) for dg in range(1, groups)] for side in range(2)] for s in sys_x]
    right_w = [pick(wall, sys_w.right[:, i]) for i in range(my)]
    left_w = [pick(wall, sys_w.left[:, i]) for i in range(my)]
    outer_w = [gathered(sys_w, side) for side in range(2)]
    back = 2 * rows * (size - 1) + (groups - 1) * 2 * my

    for c in range(nc):
        arrived(ti.at[c, pl.ds(0, back)], r2.at[c])
        outer = []
        for s in range(2):
            pair = []
            for side in range(2):
                value = jnp.concatenate(
                    [ti[c, pl.ds(b * 2 * rows + side * rows, rows), :] for b in range(s * half, (s + 1) * half)], axis=0
                )
                for dg in range(1, groups):
                    at = 4 * my + (dg - 1) * 2 * my + s * my
                    value = value + far_x[s][side][dg - 1] * ti[c, pl.ds(at, my), :]
                pair.append(value)
            outer.append(pair)
        for i in range(mx):
            part = pl.ds(i * my, my)
            more = sys_x[0].low[i] * outer[0][0] + sys_x[0].high[i] * outer[0][1]
            bend = sys_x[1].low[i] * outer[1][0] + sys_x[1].high[i] * outer[1][1]
            moved = v[0, part, :] * more
            conv[c, part, :] = conv[c, part, :] + moved
            expl[c, part, :] = expl[c, part, :] + (viscosity * bend - (time_step * gamma_now) * moved)
        low = high = None
        for i in range(my):
            row = yrow(expl, c, i)
            et[c, i] = row
            low = right_w[i] * row if low is None else low + right_w[i] * row
            high = left_w[i] * row if high is None else high + left_w[i] * row
        gw[c, 0] = low
        gw[c, 1] = high
        for d in range(1, py):
            peer = lax.rem(wall + d, py)
            way = jnp.where(peer > wall, 0, 1)
            remote(gw.at[c, way], gwr.at[c, d - 1], sent.at[0], wr.at[c], gy=peer).start()

    def solve_w(c, _):
        for i, value in enumerate(sys_w.solve([et[c, y] for y in range(my)])):
            base[c, pl.ds(i, mx, stride=my), :] = value
        return 0

    lax.fori_loop(0, nc, solve_w, 0)
    for c in range(nc):
        arrived(gwr.at[c], wr.at[c])
        for side in range(2):
            ends_w[c, side] = total(
                [outer_w[side][0] * gw[c, 1 - side]]
                + [outer_w[side][d] * gwr[c, d - 1] for d in range(1, py)]
            )

    arrived(tally, sent.at[0])
    arrived(v, sent.at[1])

    @pl.when(me < px - 1)
    def _():
        up.wait_send()

    @pl.when(me > 0)
    def _():
        down.wait_send()


def finish(cfg, conv_in, base, ends_w, shape_w, conv, upd, built, sem):
    nc, mx, my = cfg
    writes = [pltpu.make_async_copy(conv_in.at[c], conv.at[c], sem.at[c]) for c in range(nc)]
    for write in writes:
        write.start()
    for c in range(nc):
        for i in range(mx):
            part = pl.ds(i * my, my)
            built[c, part, :] = base[c, part, :] + (
                shape_w[0] * ends_w[c, 0, pl.ds(i, 1), :] + shape_w[1] * ends_w[c, 1, pl.ds(i, 1), :]
            )
        write = pltpu.make_async_copy(built.at[c], upd.at[c], sem.at[nc + c])
        write.start()
        writes.append(write)
    for write in writes:
        write.wait()


def body(counts, velocity, conv_prev):
    px, py, pz = counts
    nc, mx, my, nz = velocity.shape
    size = 4 if px % 4 == 0 else 2
    groups = px // size
    rows = 2 * my // size
    assert pz == 2 and py > 1 and px % 2 == 0 and rows % 8 == 0 and mx % 8 == 0
    flat = (nc, mx * my, nz)
    f32 = jnp.float32
    sent = 2 * rows * (size - 1) * 2 + (groups - 1) * size * rows + (py - 1) * 5 * mx

    def vmem(*shape):
        return pltpu.VMEM(shape, f32)

    def dma(n):
        return pltpu.SemaphoreType.DMA((n,))

    def out(*shape):
        return jax.ShapeDtypeStruct(shape, f32)

    whole = pl.BlockSpec(memory_space=pltpu.VMEM)
    velocity = pltpu.with_memory_space_constraint(velocity.reshape(flat), pltpu.HBM)
    conv_prev = pltpu.with_memory_space_constraint(conv_prev.reshape(flat), pltpu.HBM)
    hbm = pl.BlockSpec(memory_space=pltpu.HBM)
    parts = pl.pallas_call(
        functools.partial(kernel, (nc, mx, my, nz, px, py, size, groups)),
        out_shape=[out(*flat), out(*flat), out(nc, 2, mx, nz), out(2, my, nz)],
        in_specs=[hbm, hbm],
        out_specs=[whole] * 4,
        scratch_shapes=[
            vmem(*flat), vmem(*flat), vmem(*flat),
            vmem(nc, 2 * my, nz), vmem(nc, 2 * my, nz),
            vmem(nc, 4 * my, nz), vmem(nc, size, 2 * rows, nz), vmem(nc, size, 2 * rows, nz),
            vmem(nc, 2, rows, nz), vmem(nc, 4 * my + (groups - 1) * 2 * my, nz),
            vmem(nc, 2, 4, mx, nz), vmem(nc, py - 1, 4, mx, nz),
            vmem(nc, my, mx, nz), vmem(*flat), vmem(*flat), vmem(*flat), vmem(nc, my, mx, nz),
            vmem(nc, 2, mx, nz), vmem(nc, py - 1, mx, nz), vmem(nc * sent, nz),
            dma(nc + 1), dma(nc), dma(nc), dma(nc), dma(nc), dma(nc), dma(2), dma(2), dma(2),
        ],
        compiler_params=pltpu.CompilerParams(
            collective_id=0, has_side_effects=True, vmem_limit_bytes=32 * 1024 * 1024
        ),
    )(velocity, conv_prev)
    conv, upd = pl.pallas_call(
        functools.partial(finish, (nc, mx, my)),
        out_shape=[out(*flat), out(*flat)],
        in_specs=[whole] * 4,
        out_specs=[hbm, hbm],
        scratch_shapes=[vmem(*flat), dma(2 * nc)],
        compiler_params=pltpu.CompilerParams(vmem_limit_bytes=16 * 1024 * 1024),
    )(*parts)
    return conv.reshape(nc, mx, my, nz), upd.reshape(nc, mx, my, nz)


def solution(mesh):
    spec = P(None, "gx", "gy", "gz")
    counts = tuple(mesh.shape[name] for name in ("gx", "gy", "gz"))
    return jax.shard_map(
        functools.partial(body, counts), mesh=mesh, in_specs=(spec, spec),
        out_specs=(spec, spec), check_vma=False,
    )
```

```python
import collections
import functools

import jax
import jax.numpy as jnp
import numpy as np
from jax import lax
from jax.experimental import pallas as pl
from jax.experimental.pallas import tpu as pltpu
from jax.sharding import PartitionSpec as P

MESH = pl.DeviceIdType.MESH
WIDE = 8
time_step = 1.0
gamma_now = 5.0 / 12.0
zeta_old = -17.0 / 60.0
viscosity = 0.1

OFF = (1.0 / 3.0, 2.0 / 11.0)
EDGE = (1.0 / 36.0, 3.0 / 44.0)
NEAR = (EDGE[0] / OFF[0], EDGE[1] / OFF[1])
MID = (12.0 / 11.0 - NEAR[1]) / OFF[1]
REST = (7.0 / 9.0 - NEAR[0], -24.0 / 11.0 - 4.0 * EDGE[1] - MID)
COMPACT = (
    (OFF[0], 1.0, {1: REST[0], -1: -REST[0]}, (EDGE[0], -EDGE[0])),
    (OFF[1], 1.0, {0: REST[1]}, (EDGE[1], EDGE[1])),
)
OUT = (1.0, viscosity)


class System:
    def __init__(self, off, mid, stencil, edges, count, m):
        n = count * m
        rho = np.zeros(n + 2)
        last = 0.0
        for j in range(n + 2):
            last = -off / (mid + off * last)
            rho[j] = last

        def u(j, ref):
            if j < 0:
                return 0.0
            if j <= ref:
                return float(np.prod(rho[j:ref]))
            return 1.0 / float(np.prod(rho[ref:j]))

        def v(j, ref):
            return u(n - 1 - j, n - 1 - ref)

        def inv(i, j):
            low = rho[i - 1] if i > 0 else 0.0
            high = rho[n - 2 - i] if i < n - 1 else 0.0
            diag = 1.0 / (mid + off * low + off * high)
            return diag * (u(j, i) if j <= i else v(j, i))

        def b(j, col):
            extra = edges[0] if j == col == 0 else edges[1] if j == col == n - 1 else 0.0
            return stencil.get(col - j, 0.0) + extra

        self.off, self.m, self.count = off, m, count
        self.right, self.left = np.zeros((count, m)), np.zeros((count, m))
        self.fix_low, self.fix_high = np.zeros(count), np.zeros(count)
        self.edge_low, self.edge_high = np.zeros(count), np.zeros(count)
        self.edge_low[0], self.edge_high[-1] = edges
        self.d = np.zeros((count, 4))
        self.t = np.zeros((count, 2))
        self.weights = np.zeros((2, count, 2, count))
        for p in range(count):
            start, end = p * m, p * m + m - 1
            for k in range(m):
                col = start + k
                rows = [j for j in range(col - 2, col + 3) if 0 <= j < n]
                self.right[p, k] = sum(u(j, end) * b(j, col) for j in rows)
                self.left[p, k] = sum(v(j, start) * b(j, col) for j in rows)
            if p > 0:
                e = start - 1
                self.fix_low[p] = (inv(e, e + 1) - inv(e, e) * u(e + 1, e)) * b(e + 1, e)
                self.d[p, 0], self.d[p, 1] = inv(e, e), inv(e, e + 1)
                self.t[p, 0] = u(e, end)
                for q in range(count):
                    if q < p:
                        self.weights[0, q, 0, p] = inv(e, q * m + m - 1)
                    else:
                        self.weights[0, q, 1, p] = inv(e, q * m)
            if p < count - 1:
                f = end + 1
                self.fix_high[p] = (inv(f, f - 1) - inv(f, f) * v(f - 1, f)) * b(f - 1, f)
                self.d[p, 2], self.d[p, 3] = inv(f, f - 1), inv(f, f)
                self.t[p, 1] = v(f, start)
                for q in range(count):
                    if q > p:
                        self.weights[1, q, 1, p] = inv(f, q * m)
                    else:
                        self.weights[1, q, 0, p] = inv(f, q * m + m - 1)
        pivots, ratios, last = [], [], 0.0
        for _ in range(m):
            pivot = mid - off * last
            last = off / pivot
            pivots.append(pivot)
            ratios.append(last)
        self.scale = [float(1.0 / pivot) for pivot in pivots]
        self.ratio = [float(ratio) for ratio in ratios]
        unit = np.zeros(m)
        unit[0] = 1.0
        self.low = [-off * value for value in self.solve(list(unit))]
        self.high = self.low[::-1]

    def solve(self, rows):
        return self.sweep([row * self.scale[i] for i, row in enumerate(rows)])

    def sweep(self, scaled):
        done, carry = [], None
        for i, fresh in enumerate(scaled):
            carry = fresh if carry is None else fresh - self.ratio[i] * carry
            done.append(carry)
        for i in range(self.m - 2, -1, -1):
            done[i] = done[i] - self.ratio[i] * done[i + 1]
        return done


def pick(place, values):
    values = [float(np.float32(value)) for value in values]
    common = collections.Counter(values).most_common(1)[0][0]
    result = jnp.float32(common)
    for index, value in enumerate(values):
        if value != common:
            result = jnp.where(place == index, jnp.float32(value), result)
    return result


def line(systems, cells, low, high):
    m = len(cells) - 2
    odd = [cells[i + 2] - cells[i] for i in range(m)]
    even = [cells[i + 2] + cells[i] for i in range(m)]
    solved = []
    for s in range(2):
        system = systems[s]
        source = odd if s == 0 else cells[1:-1]
        scaled = [(REST[s] * OUT[s] * system.scale[i]) * source[i] for i in range(m)]
        scaled[0] = scaled[0] + low[s] * system.scale[0]
        scaled[m - 1] = scaled[m - 1] + high[s] * system.scale[m - 1]
        solved.append(system.sweep(scaled))
    first = [solved[0][i] + NEAR[0] * odd[i] for i in range(m)]
    second = [
        solved[1][i] + ((NEAR[1] * viscosity) * even[i] + (MID * viscosity) * cells[i + 1]) for i in range(m)
    ]
    return first, second


def total(terms):
    return functools.reduce(lambda a, b: a + b, terms)


def kernel(
    cfg, v_hbm, cp_hbm, conv, base, ends_w, shape_w,
    v, cp, zo, xlo, xhi, gx, gr, to, st, ti, yout, yin, vt, fy, sy, expl, et, gw, gwr, tally,
    load, r1, r2, yr, zr, wr, hs, hr, sent,
):
    nc, mx, my, nz, px, py, size, groups = cfg
    rows = 2 * my // size
    me = lax.axis_index("gx")
    wall = lax.axis_index("gy")
    core = lax.axis_index("gz")
    group, rank = me // size, lax.rem(me, size)
    sys_x = [System(*pair, px, mx) for pair in COMPACT]
    sys_y = [System(*pair, py, my) for pair in COMPACT]
    beta = 4.0 * my * my
    sys_w = System(-beta, 1.0 + 2.0 * beta, {0: 1.0}, (0.0, 0.0), py, my)

    barrier = pltpu.get_barrier_semaphore()
    for d in range(1, px):
        pl.semaphore_signal(barrier, inc=1, device_id={"gx": lax.rem(me + d, px)}, device_id_type=MESH)
    for d in range(1, py):
        pl.semaphore_signal(barrier, inc=1, device_id={"gy": lax.rem(wall + d, py)}, device_id_type=MESH)
    pl.semaphore_signal(barrier, inc=1, device_id={"gz": 1 - core}, device_id_type=MESH)

    reads = [pltpu.make_async_copy(v_hbm.at[c], v.at[c], load.at[c]) for c in range(nc)]
    reads.append(pltpu.make_async_copy(cp_hbm, cp, load.at[nc]))
    for read in reads:
        read.start()

    def remote(src, dst, send, recv, **target):
        return pltpu.make_async_remote_copy(
            src_ref=src, dst_ref=dst, send_sem=send, recv_sem=recv,
            device_id=target, device_id_type=MESH,
        )

    def arrived(ref, sem):
        pltpu.make_async_copy(ref, ref, sem).wait()

    def other(d):
        if size & (size - 1):
            return lax.rem(rank + d, size)
        result, bit = 0, 1
        while bit < size:
            mine = lax.rem(rank // bit, 2)
            result = result + bit * ((1 - mine) if d & bit else mine)
            bit *= 2
        return result

    weigh_x = [
        [[pick(me, table[:, i]) for i in range(mx)] for table in (s.right, s.left)] for s in sys_x
    ]

    def sums_x(c):
        def step(b, _):
            part = [v[c, pl.ds(pl.multiple_of(i * my + b * 8, 8), 8), :] for i in range(mx)]
            for s in range(2):
                for way in range(2):
                    value = total([weigh_x[s][way][i] * part[i] for i in range(mx)])
                    flat = s * my + b * 8
                    owner = flat // rows
                    at = owner * 2 * rows + way * rows + lax.rem(flat, rows)
                    gx[c, pl.ds(pl.multiple_of(at, 8), 8), :] = value
            return 0

        lax.fori_loop(0, my // 8, step, 0)

    own = pl.ds(pl.multiple_of(rank * 2 * rows, 8), 2 * rows)
    for c in range(nc):
        reads[c].wait()
        sums_x(c)
        if c == 0:
            pl.semaphore_wait(barrier, px - 1 + py - 1 + 1)
        for d in range(size - 1, 0, -1):
            t = other(d)
            remote(
                gx.at[c, pl.ds(pl.multiple_of(t * 2 * rows, 8), 2 * rows)], gr.at[c, rank],
                sent.at[0], r1.at[c], gx=group * size + t,
            ).start()
        gr[c, rank] = gx[c, own, :]
        remote(v.at[c], zo.at[c], sent.at[1], zr.at[c], gz=1 - core).start()

    up = remote(v.at[:, pl.ds((mx - 1) * my, my)], xlo, hs.at[0], hr.at[0], gx=lax.rem(me + 1, px))
    down = remote(v.at[:, pl.ds(0, my)], xhi, hs.at[1], hr.at[1], gx=lax.rem(me + px - 1, px))

    @pl.when(me < px - 1)
    def _():
        up.start()

    @pl.when(me > 0)
    def _():
        down.start()

    def yrow(ref, c, y):
        return ref[c, pl.ds(y, mx, stride=my), :]

    weigh_y = [
        [[pick(wall, table[:, i]) for i in range(my)] for table in (s.right, s.left)] for s in sys_y
    ]

    def sums_y(c, _):
        sums = [[None, None], [None, None]]
        for i in range(my):
            row = yrow(v, c, i)
            vt[c, i] = row
            if i == 0:
                yout[c, 1, 0] = row
            if i == my - 1:
                yout[c, 0, 0] = row
            for s in range(2):
                for way in range(2):
                    term = weigh_y[s][way][i] * row
                    sums[s][way] = term if i == 0 else sums[s][way] + term
        for s in range(2):
            for way in range(2):
                yout[c, way, 1 + s] = sums[s][way]
        for d in range(1, py):
            peer = lax.rem(wall + d, py)
            way = jnp.where(peer > wall, 0, 1)
            remote(yout.at[c, way], yin.at[c, d - 1], sent.at[0], yr.at[c], gy=peer).start()
        return 0

    for c in range(nc):
        sums_y(c, 0)

    for i in range(my):
        shape_w[0, pl.ds(i, 1), :] = jnp.full((1, nz), sys_w.low[i], jnp.float32)
        shape_w[1, pl.ds(i, 1), :] = jnp.full((1, nz), sys_w.high[i], jnp.float32)

    slab = min(128, mx * my)
    lane = lax.broadcasted_iota(jnp.int32, (slab, nz), 1)
    reads[nc].wait()

    def solve_z(c):
        def step(index, _):
            part = pl.ds(pl.multiple_of(index * slab, slab), slab)
            mine, rest = v[c, part, :], zo[c, part, :]

            def after(k):
                return pltpu.roll(jnp.where(lane < k, rest, mine), nz - k, 1)

            def before(k):
                return pltpu.roll(jnp.where(lane >= nz - k, rest, mine), k, 1)

            high, low = [after(k) for k in (1, 2, 3)], [before(k) for k in (1, 2, 3)]
            odd = [a - b for a, b in zip(high, low)]
            even = [a + b for a, b in zip(high, low)]
            first = (45.0 / 60.0) * odd[0] - (9.0 / 60.0) * odd[1] + (1.0 / 60.0) * odd[2]
            bend = (
                (viscosity * 2.0 / 180.0) * even[2] - (viscosity * 27.0 / 180.0) * even[1]
                + (viscosity * 270.0 / 180.0) * even[0] + (1.0 - viscosity * 490.0 / 180.0) * mine
            )
            conv[c, part, :] = v[2, part, :] * first
            expl[c, part, :] = bend - (time_step * zeta_old) * cp[c, part, :]
            return 0

        arrived(zo.at[c], zr.at[c])
        lax.fori_loop(0, mx * my // slab, step, 0)

    half = size // 2
    share = rank // half

    def table(field):
        return [
            pick(group * 2 + share, [field(sys_x[s], g * size + m) for g in range(groups) for s in range(2)])
            for m in range(size)
        ]

    t0, t1 = (table(lambda s, p, k=k: s.t[p, k]) for k in range(2))
    d0, d1, d2, d3 = (table(lambda s, p, k=k: s.d[p, k]) for k in range(4))

    def exchange(c):
        arrived(gr.at[c, pl.ds(0, size - 1)], r1.at[c])
        below, above = [None] * size, [None] * size
        for m in range(size):
            here = gr[c, m, pl.ds(0, rows), :]
            below[m] = here if m == 0 else here + t0[m] * below[m - 1]
        for m in reversed(range(size)):
            here = gr[c, m, pl.ds(rows, rows), :]
            above[m] = here if m == size - 1 else here + t1[m] * above[m + 1]
        if groups > 1:
            st[c, 0] = below[size - 1]
            st[c, 1] = above[0]
            for dg in range(1, groups):
                there = lax.rem(group + dg, groups)
                way = jnp.where(there > group, 0, 1)
                at = pl.multiple_of(4 * my + (dg - 1) * 2 * my + rank * rows, 8)
                for d in range(size - 1, -1, -1):
                    m = other(d)
                    remote(
                        st.at[c, way], ti.at[c, pl.ds(at, rows)], sent.at[0], r2.at[c],
                        gx=there * size + m,
                    ).start()
        for m in range(size):
            low = d1[m] * above[m]
            to[c, m, pl.ds(0, rows), :] = low if m == 0 else low + d0[m] * below[m - 1]
            high = d2[m] * below[m]
            to[c, m, pl.ds(rows, rows), :] = high if m == size - 1 else high + d3[m] * above[m + 1]
        for d in range(size - 1, 0, -1):
            t = other(d)
            remote(to.at[c, t], ti.at[c, own], sent.at[0], r2.at[c], gx=group * size + t).start()
        ti[c, own, :] = to[c, rank]

    def gathered(system, side, by=1.0):
        def way(q, p):
            return 1 - side if q == p else (0 if q < p else 1)

        return [
            pick(wall, [by * system.weights[side, (p - d) % py, way((p - d) % py, p), p] for p in range(py)])
            for d in range(py)
        ]

    def side_of(systems, place, out):
        return [
            (
                pick(place, -out[s] * system.off * system.fix_low), pick(place, out[s] * system.edge_low),
                pick(place, -out[s] * system.off * system.fix_high), pick(place, out[s] * system.edge_high),
            )
            for s, system in enumerate(systems)
        ]

    near_y = side_of(sys_y, wall, OUT)
    outer_y = [[gathered(s, side, -OUT[k] * s.off) for side in range(2)] for k, s in enumerate(sys_y)]
    wide = WIDE

    def solve_y(index, _):
        c = index // (mx // wide)
        first_row = pl.multiple_of(lax.rem(index, mx // wide) * wide, wide)
        part = pl.ds(first_row, wide)
        cells = [jnp.where(wall > 0, yin[c, 0, 0, part, :], 0.0)]
        cells += [vt[c, y, part, :] for y in range(my)]
        cells += [jnp.where(wall < py - 1, yin[c, py - 2, 0, part, :], 0.0)]
        more = [
            [
                total(
                    [outer_y[s][side][0] * yout[c, 1 - side, 1 + s, part, :]]
                    + [outer_y[s][side][d] * yin[c, d - 1, 1 + s, part, :] for d in range(1, py)]
                    + [near_y[s][2 * side] * cells[0 - side], near_y[s][2 * side + 1] * cells[1 if side == 0 else my]]
                )
                for s in range(2)
            ]
            for side in range(2)
        ]
        for values, out in zip(line(sys_y, cells, *more), (fy, sy)):
            for i, value in enumerate(values):
                out[c, pl.ds(first_row * my + i, wide, stride=my), :] = value
        return 0

    near_x = side_of(sys_x, me, OUT)
    tile = 16 if my % 16 == 0 else 8

    def solve_x(index, _):
        c = index // (my // tile)
        start = pl.multiple_of(lax.rem(index, my // tile) * tile, tile)
        cells = [xlo[c, pl.ds(start, tile), :]]
        cells += [v[c, pl.ds(i * my + start, tile), :] for i in range(mx)]
        cells += [xhi[c, pl.ds(start, tile), :]]
        more = [
            [near_x[s][2 * side] * cells[0 - side] + near_x[s][2 * side + 1] * cells[1 if side == 0 else mx] for s in range(2)]
            for side in range(2)
        ]
        first, second = line(sys_x, cells, *more)
        for i in range(mx):
            part = pl.ds(i * my + start, tile)
            conv[c, part, :] = conv[c, part, :] + (v[0, part, :] * first[i] + v[1, part, :] * fy[c, part, :])
            expl[c, part, :] = expl[c, part, :] + (second[i] + sy[c, part, :])
        return 0

    solve_z(0)
    for c in range(nc):
        exchange(c)
    for c in range(1, nc):
        solve_z(c)
    for c in range(nc):
        arrived(yin.at[c], yr.at[c])
    lax.fori_loop(0, nc * (mx // wide), solve_y, 0)

    @pl.when(me > 0)
    def _():
        up.wait_recv()

    @pl.when(me == 0)
    def _():
        xlo[...] = jnp.zeros_like(xlo)

    @pl.when(me < px - 1)
    def _():
        down.wait_recv()

    @pl.when(me == px - 1)
    def _():
        xhi[...] = jnp.zeros_like(xhi)

    lax.fori_loop(0, nc * (my // tile), solve_x, 0)

    def far(s, side, dg):
        values = []
        for p in range(px):
            g, q = p // size, (p // size - dg) % groups
            if q < g:
                value = s.d[p, 2 * side]
                for k in range((q + 1) * size, p + side):
                    value = value * s.t[k, 0]
            else:
                value = s.d[p, 2 * side + 1]
                for k in range(p + side, q * size):
                    value = value * s.t[k, 1]
            values.append(value)
        return pick(me, values)

    far_x = [[[far(s, side, dg) for dg in range(1, groups)] for side in range(2)] for s in sys_x]
    right_w = [pick(wall, sys_w.right[:, i]) for i in range(my)]
    left_w = [pick(wall, sys_w.left[:, i]) for i in range(my)]
    outer_w = [gathered(sys_w, side) for side in range(2)]
    back = 2 * rows * (size - 1) + (groups - 1) * 2 * my

    for c in range(nc):
        arrived(ti.at[c, pl.ds(0, back)], r2.at[c])
        outer = []
        for s in range(2):
            pair = []
            for side in range(2):
                value = jnp.concatenate(
                    [ti[c, pl.ds(b * 2 * rows + side * rows, rows), :] for b in range(s * half, (s + 1) * half)], axis=0
                )
                for dg in range(1, groups):
                    at = 4 * my + (dg - 1) * 2 * my + s * my
                    value = value + far_x[s][side][dg - 1] * ti[c, pl.ds(at, my), :]
                pair.append(value)
            outer.append(pair)
        for i in range(mx):
            part = pl.ds(i * my, my)
            more = sys_x[0].low[i] * outer[0][0] + sys_x[0].high[i] * outer[0][1]
            bend = (viscosity * sys_x[1].low[i]) * outer[1][0] + (viscosity * sys_x[1].high[i]) * outer[1][1]
            moved = conv[c, part, :] + v[0, part, :] * more
            conv[c, part, :] = moved
            expl[c, part, :] = expl[c, part, :] + (bend - (time_step * gamma_now) * moved)
        low = high = None
        for i in range(my):
            row = yrow(expl, c, i)
            et[c, i] = row
            low = right_w[i] * row if low is None else low + right_w[i] * row
            high = left_w[i] * row if high is None else high + left_w[i] * row
        gw[c, 0] = low
        gw[c, 1] = high
        for d in range(1, py):
            peer = lax.rem(wall + d, py)
            way = jnp.where(peer > wall, 0, 1)
            remote(gw.at[c, way], gwr.at[c, d - 1], sent.at[0], wr.at[c], gy=peer).start()

    def solve_w(c, _):
        for i, value in enumerate(sys_w.solve([et[c, y] for y in range(my)])):
            base[c, pl.ds(i, mx, stride=my), :] = value
        return 0

    lax.fori_loop(0, nc, solve_w, 0)
    for c in range(nc):
        arrived(gwr.at[c], wr.at[c])
        for side in range(2):
            ends_w[c, side] = total(
                [outer_w[side][0] * gw[c, 1 - side]]
                + [outer_w[side][d] * gwr[c, d - 1] for d in range(1, py)]
            )

    arrived(tally, sent.at[0])
    arrived(v, sent.at[1])

    @pl.when(me < px - 1)
    def _():
        up.wait_send()

    @pl.when(me > 0)
    def _():
        down.wait_send()


def finish(cfg, conv_in, base, ends_w, shape_w, conv, upd, built, sem):
    nc, mx, my = cfg
    writes = [pltpu.make_async_copy(conv_in.at[c], conv.at[c], sem.at[c]) for c in range(nc)]
    for write in writes:
        write.start()
    for c in range(nc):
        for i in range(mx):
            part = pl.ds(i * my, my)
            built[c, part, :] = base[c, part, :] + (
                shape_w[0] * ends_w[c, 0, pl.ds(i, 1), :] + shape_w[1] * ends_w[c, 1, pl.ds(i, 1), :]
            )
        write = pltpu.make_async_copy(built.at[c], upd.at[c], sem.at[nc + c])
        write.start()
        writes.append(write)
    for write in writes:
        write.wait()


def body(counts, velocity, conv_prev):
    px, py, pz = counts
    nc, mx, my, nz = velocity.shape
    size = 4 if px % 4 == 0 else 2
    groups = px // size
    rows = 2 * my // size
    assert pz == 2 and py > 1 and px % 2 == 0 and rows % 8 == 0 and mx % 8 == 0
    flat = (nc, mx * my, nz)
    f32 = jnp.float32
    sent = 2 * rows * (size - 1) * 2 + (groups - 1) * size * rows + (py - 1) * 4 * mx

    def vmem(*shape):
        return pltpu.VMEM(shape, f32)

    def dma(n):
        return pltpu.SemaphoreType.DMA((n,))

    def out(*shape):
        return jax.ShapeDtypeStruct(shape, f32)

    whole = pl.BlockSpec(memory_space=pltpu.VMEM)
    velocity = pltpu.with_memory_space_constraint(velocity.reshape(flat), pltpu.HBM)
    conv_prev = pltpu.with_memory_space_constraint(conv_prev.reshape(flat), pltpu.HBM)
    hbm = pl.BlockSpec(memory_space=pltpu.HBM)
    parts = pl.pallas_call(
        functools.partial(kernel, (nc, mx, my, nz, px, py, size, groups)),
        out_shape=[out(*flat), out(*flat), out(nc, 2, mx, nz), out(2, my, nz)],
        in_specs=[hbm, hbm],
        out_specs=[whole] * 4,
        scratch_shapes=[
            vmem(*flat), vmem(*flat), vmem(*flat),
            vmem(nc, my, nz), vmem(nc, my, nz),
            vmem(nc, 4 * my, nz), vmem(nc, size, 2 * rows, nz), vmem(nc, size, 2 * rows, nz),
            vmem(nc, 2, rows, nz), vmem(nc, 4 * my + (groups - 1) * 2 * my, nz),
            vmem(nc, 2, 3, mx, nz), vmem(nc, py - 1, 3, mx, nz),
            vmem(nc, my, mx, nz), vmem(*flat), vmem(*flat), vmem(*flat), vmem(nc, my, mx, nz),
            vmem(nc, 2, mx, nz), vmem(nc, py - 1, mx, nz), vmem(nc * sent, nz),
            dma(nc + 1), dma(nc), dma(nc), dma(nc), dma(nc), dma(nc), dma(2), dma(2), dma(2),
        ],
        compiler_params=pltpu.CompilerParams(
            collective_id=0, has_side_effects=True, vmem_limit_bytes=32 * 1024 * 1024
        ),
    )(velocity, conv_prev)
    conv, upd = pl.pallas_call(
        functools.partial(finish, (nc, mx, my)),
        out_shape=[out(*flat), out(*flat)],
        in_specs=[whole] * 4,
        out_specs=[hbm, hbm],
        scratch_shapes=[vmem(*flat), dma(2 * nc)],
        compiler_params=pltpu.CompilerParams(vmem_limit_bytes=16 * 1024 * 1024),
    )(*parts)
    return conv.reshape(nc, mx, my, nz), upd.reshape(nc, mx, my, nz)


def solution(mesh):
    spec = P(None, "gx", "gy", "gz")
    counts = tuple(mesh.shape[name] for name in ("gx", "gy", "gz"))
    return jax.shard_map(
        functools.partial(body, counts), mesh=mesh, in_specs=(spec, spec),
        out_specs=(spec, spec), check_vma=False,
    )
```

```python
import collections
import functools

import jax
import jax.numpy as jnp
import numpy as np
from jax import lax
from jax.experimental import pallas as pl
from jax.experimental.pallas import tpu as pltpu
from jax.sharding import PartitionSpec as P

MESH = pl.DeviceIdType.MESH
WIDE = 8
time_step = 1.0
gamma_now = 5.0 / 12.0
zeta_old = -17.0 / 60.0
viscosity = 0.1

OFF = (1.0 / 3.0, 2.0 / 11.0)
EDGE = (1.0 / 36.0, 3.0 / 44.0)
NEAR = (EDGE[0] / OFF[0], EDGE[1] / OFF[1])
MID = (12.0 / 11.0 - NEAR[1]) / OFF[1]
REST = (7.0 / 9.0 - NEAR[0], -24.0 / 11.0 - 4.0 * EDGE[1] - MID)
COMPACT = (
    (OFF[0], 1.0, {1: REST[0], -1: -REST[0]}, (EDGE[0], -EDGE[0])),
    (OFF[1], 1.0, {0: REST[1]}, (EDGE[1], EDGE[1])),
)
OUT = (1.0, viscosity)


class System:
    def __init__(self, off, mid, stencil, edges, count, m):
        n = count * m
        rho = np.zeros(n + 2)
        last = 0.0
        for j in range(n + 2):
            last = -off / (mid + off * last)
            rho[j] = last

        def u(j, ref):
            if j < 0:
                return 0.0
            if j <= ref:
                return float(np.prod(rho[j:ref]))
            return 1.0 / float(np.prod(rho[ref:j]))

        def v(j, ref):
            return u(n - 1 - j, n - 1 - ref)

        def inv(i, j):
            low = rho[i - 1] if i > 0 else 0.0
            high = rho[n - 2 - i] if i < n - 1 else 0.0
            diag = 1.0 / (mid + off * low + off * high)
            return diag * (u(j, i) if j <= i else v(j, i))

        def b(j, col):
            extra = edges[0] if j == col == 0 else edges[1] if j == col == n - 1 else 0.0
            return stencil.get(col - j, 0.0) + extra

        self.off, self.m, self.count = off, m, count
        self.right, self.left = np.zeros((count, m)), np.zeros((count, m))
        self.fix_low, self.fix_high = np.zeros(count), np.zeros(count)
        self.edge_low, self.edge_high = np.zeros(count), np.zeros(count)
        self.edge_low[0], self.edge_high[-1] = edges
        self.d = np.zeros((count, 4))
        self.t = np.zeros((count, 2))
        self.weights = np.zeros((2, count, 2, count))
        for p in range(count):
            start, end = p * m, p * m + m - 1
            for k in range(m):
                col = start + k
                rows = [j for j in range(col - 2, col + 3) if 0 <= j < n]
                self.right[p, k] = sum(u(j, end) * b(j, col) for j in rows)
                self.left[p, k] = sum(v(j, start) * b(j, col) for j in rows)
            if p > 0:
                e = start - 1
                self.fix_low[p] = (inv(e, e + 1) - inv(e, e) * u(e + 1, e)) * b(e + 1, e)
                self.d[p, 0], self.d[p, 1] = inv(e, e), inv(e, e + 1)
                self.t[p, 0] = u(e, end)
                for q in range(count):
                    if q < p:
                        self.weights[0, q, 0, p] = inv(e, q * m + m - 1)
                    else:
                        self.weights[0, q, 1, p] = inv(e, q * m)
            if p < count - 1:
                f = end + 1
                self.fix_high[p] = (inv(f, f - 1) - inv(f, f) * v(f - 1, f)) * b(f - 1, f)
                self.d[p, 2], self.d[p, 3] = inv(f, f - 1), inv(f, f)
                self.t[p, 1] = v(f, start)
                for q in range(count):
                    if q > p:
                        self.weights[1, q, 1, p] = inv(f, q * m)
                    else:
                        self.weights[1, q, 0, p] = inv(f, q * m + m - 1)
        pivots, ratios, last = [], [], 0.0
        for _ in range(m):
            pivot = mid - off * last
            last = off / pivot
            pivots.append(pivot)
            ratios.append(last)
        self.scale = [float(1.0 / pivot) for pivot in pivots]
        self.ratio = [float(ratio) for ratio in ratios]
        unit = np.zeros(m)
        unit[0] = 1.0
        self.low = [-off * value for value in self.solve(list(unit))]
        self.high = self.low[::-1]

    def solve(self, rows):
        return self.sweep([row * self.scale[i] for i, row in enumerate(rows)])

    def sweep(self, scaled):
        done, carry = [], None
        for i, fresh in enumerate(scaled):
            carry = fresh if carry is None else fresh - self.ratio[i] * carry
            done.append(carry)
        for i in range(self.m - 2, -1, -1):
            done[i] = done[i] - self.ratio[i] * done[i + 1]
        return done


def pick(place, values):
    values = [float(np.float32(value)) for value in values]
    common = collections.Counter(values).most_common(1)[0][0]
    result = jnp.float32(common)
    for index, value in enumerate(values):
        if value != common:
            result = jnp.where(place == index, jnp.float32(value), result)
    return result


def line(systems, cells, low, high):
    m = len(cells) - 2
    odd = [cells[i + 2] - cells[i] for i in range(m)]
    even = [cells[i + 2] + cells[i] for i in range(m)]
    solved = []
    for s in range(2):
        system = systems[s]
        source = odd if s == 0 else cells[1:-1]
        scaled = [(REST[s] * OUT[s] * system.scale[i]) * source[i] for i in range(m)]
        scaled[0] = scaled[0] + low[s] * system.scale[0]
        scaled[m - 1] = scaled[m - 1] + high[s] * system.scale[m - 1]
        solved.append(system.sweep(scaled))
    first = [solved[0][i] + NEAR[0] * odd[i] for i in range(m)]
    second = [
        solved[1][i] + ((NEAR[1] * viscosity) * even[i] + (MID * viscosity) * cells[i + 1]) for i in range(m)
    ]
    return first, second


def total(terms):
    return functools.reduce(lambda a, b: a + b, terms)


def kernel(
    cfg, v_hbm, cp_hbm, conv, base, ends_w, shape_w,
    v, cp, zo, xlo, xhi, gx, gr, to, st, ti, yout, yin, vt, fy, sy, expl, et, gw, gwr, tally,
    load, r1, r2, yr, zr, wr, hs, hr, sent,
):
    nc, mx, my, nz, px, py, size, groups = cfg
    rows = 2 * my // size
    me = lax.axis_index("gx")
    wall = lax.axis_index("gy")
    core = lax.axis_index("gz")
    group, rank = me // size, lax.rem(me, size)
    sys_x = [System(*pair, px, mx) for pair in COMPACT]
    sys_y = [System(*pair, py, my) for pair in COMPACT]
    beta = 4.0 * my * my
    sys_w = System(-beta, 1.0 + 2.0 * beta, {0: 1.0}, (0.0, 0.0), py, my)

    barrier = pltpu.get_barrier_semaphore()

    def greet(**device):
        pl.semaphore_signal(barrier, inc=1, device_id=device, device_id_type=MESH)

    for d in range(1, size):
        greet(gx=group * size + lax.rem(rank + d, size))
    for d in range(1, groups):
        greet(gx=lax.rem(group + d, groups) * size + rank)
    for d in range(1, py):
        greet(gy=lax.rem(wall + d, py))
    greet(gz=1 - core)
    is_last = (rank == size - 1) & (me < px - 1)
    is_first = (rank == 0) & (me > 0)

    @pl.when(is_last)
    def _():
        greet(gx=me + 1)

    @pl.when(is_first)
    def _():
        greet(gx=me - 1)

    reads = [pltpu.make_async_copy(v_hbm.at[c], v.at[c], load.at[c]) for c in range(nc)]
    reads.append(pltpu.make_async_copy(cp_hbm, cp, load.at[nc]))
    for read in reads:
        read.start()

    def remote(src, dst, send, recv, **target):
        return pltpu.make_async_remote_copy(
            src_ref=src, dst_ref=dst, send_sem=send, recv_sem=recv,
            device_id=target, device_id_type=MESH,
        )

    def arrived(ref, sem):
        pltpu.make_async_copy(ref, ref, sem).wait()

    def other(d, flip=False):
        if size & (size - 1):
            return lax.rem(rank + d, size)
        result, bit = 0, 1
        while bit < size:
            mine = lax.rem(rank // bit, 2)
            if bit == 1 and flip:
                mine = lax.rem(mine + core, 2)
            result = result + bit * ((1 - mine) if d & bit else mine)
            bit *= 2
        return result

    weigh_x = [
        [[pick(me, table[:, i]) for i in range(mx)] for table in (s.right, s.left)] for s in sys_x
    ]

    def sums_x(c):
        def step(b, _):
            part = [v[c, pl.ds(pl.multiple_of(i * my + b * 8, 8), 8), :] for i in range(mx)]
            for s in range(2):
                for way in range(2):
                    value = total([weigh_x[s][way][i] * part[i] for i in range(mx)])
                    flat = s * my + b * 8
                    owner = flat // rows
                    at = owner * 2 * rows + way * rows + lax.rem(flat, rows)
                    gx[c, pl.ds(pl.multiple_of(at, 8), 8), :] = value
            return 0

        lax.fori_loop(0, my // 8, step, 0)

    own = pl.ds(pl.multiple_of(rank * 2 * rows, 8), 2 * rows)
    for c in range(nc):
        reads[c].wait()
        sums_x(c)
        if c == 0:
            pl.semaphore_wait(
                barrier, size - 1 + groups - 1 + py - 1 + 1 + jnp.where(is_last | is_first, 1, 0)
            )
        for d in range(size - 1, 0, -1):
            t = other(d, d > 1)
            remote(
                gx.at[c, pl.ds(pl.multiple_of(t * 2 * rows, 8), 2 * rows)], gr.at[c, rank],
                sent.at[0], r1.at[c], gx=group * size + t,
            ).start()
        gr[c, rank] = gx[c, own, :]
        remote(v.at[c], zo.at[c], sent.at[1], zr.at[c], gz=1 - core).start()

    up = remote(v.at[:, pl.ds((mx - 1) * my, my)], xlo, hs.at[0], hr.at[0], gx=lax.rem(me + 1, px))
    down = remote(v.at[:, pl.ds(0, my)], xhi, hs.at[1], hr.at[1], gx=lax.rem(me + px - 1, px))

    @pl.when(me < px - 1)
    def _():
        up.start()

    @pl.when(me > 0)
    def _():
        down.start()

    def yrow(ref, c, y):
        return ref[c, pl.ds(y, mx, stride=my), :]

    weigh_y = [
        [[pick(wall, table[:, i]) for i in range(my)] for table in (s.right, s.left)] for s in sys_y
    ]

    def sums_y(c, _):
        sums = [[None, None], [None, None]]
        for i in range(my):
            row = yrow(v, c, i)
            vt[c, i] = row
            if i == 0:
                yout[c, 1, 0] = row
            if i == my - 1:
                yout[c, 0, 0] = row
            for s in range(2):
                for way in range(2):
                    term = weigh_y[s][way][i] * row
                    sums[s][way] = term if i == 0 else sums[s][way] + term
        for s in range(2):
            for way in range(2):
                yout[c, way, 1 + s] = sums[s][way]
        for d in range(1, py):
            peer = lax.rem(wall + d, py)
            way = jnp.where(peer > wall, 0, 1)
            remote(yout.at[c, way], yin.at[c, d - 1], sent.at[0], yr.at[c], gy=peer).start()
        return 0

    for c in range(nc):
        sums_y(c, 0)

    for i in range(my):
        shape_w[0, pl.ds(i, 1), :] = jnp.full((1, nz), sys_w.low[i], jnp.float32)
        shape_w[1, pl.ds(i, 1), :] = jnp.full((1, nz), sys_w.high[i], jnp.float32)

    slab = mx * my
    lane = lax.broadcasted_iota(jnp.int32, (slab, nz), 1)
    reads[nc].wait()

    def solve_z(c):
        def step(index, _):
            part = pl.ds(pl.multiple_of(index * slab, slab), slab)
            mine, rest = v[c, part, :], zo[c, part, :]

            def after(k):
                return pltpu.roll(jnp.where(lane < k, rest, mine), nz - k, 1)

            def before(k):
                return pltpu.roll(jnp.where(lane >= nz - k, rest, mine), k, 1)

            high, low = [after(k) for k in (1, 2, 3)], [before(k) for k in (1, 2, 3)]
            odd = [a - b for a, b in zip(high, low)]
            even = [a + b for a, b in zip(high, low)]
            first = (45.0 / 60.0) * odd[0] - (9.0 / 60.0) * odd[1] + (1.0 / 60.0) * odd[2]
            bend = (
                (viscosity * 2.0 / 180.0) * even[2] - (viscosity * 27.0 / 180.0) * even[1]
                + (viscosity * 270.0 / 180.0) * even[0] + (1.0 - viscosity * 490.0 / 180.0) * mine
            )
            conv[c, part, :] = v[2, part, :] * first
            expl[c, part, :] = bend - (time_step * zeta_old) * cp[c, part, :]
            return 0

        arrived(zo.at[c], zr.at[c])
        lax.fori_loop(0, mx * my // slab, step, 0)

    half = size // 2
    share = rank // half

    def table(field):
        return [
            pick(group * 2 + share, [field(sys_x[s], g * size + m) for g in range(groups) for s in range(2)])
            for m in range(size)
        ]

    t0, t1 = (table(lambda s, p, k=k: s.t[p, k]) for k in range(2))
    d0, d1, d2, d3 = (table(lambda s, p, k=k: s.d[p, k]) for k in range(4))

    def exchange(c):
        arrived(gr.at[c, pl.ds(0, size - 1)], r1.at[c])
        below, above = [None] * size, [None] * size
        for m in range(size):
            here = gr[c, m, pl.ds(0, rows), :]
            below[m] = here if m == 0 else here + t0[m] * below[m - 1]
        for m in reversed(range(size)):
            here = gr[c, m, pl.ds(rows, rows), :]
            above[m] = here if m == size - 1 else here + t1[m] * above[m + 1]
        if groups > 1:
            st[c, 0] = below[size - 1]
            st[c, 1] = above[0]
            for dg in range(1, groups):
                there = lax.rem(group + dg, groups)
                way = jnp.where(there > group, 0, 1)
                at = pl.multiple_of(4 * my + (dg - 1) * 2 * my + rank * rows, 8)
                for d in range(size - 1, -1, -1):
                    m = other(d, True)
                    remote(
                        st.at[c, way], ti.at[c, pl.ds(at, rows)], sent.at[0], r2.at[c],
                        gx=there * size + m,
                    ).start()
        for m in range(size):
            low = d1[m] * above[m]
            to[c, m, pl.ds(0, rows), :] = low if m == 0 else low + d0[m] * below[m - 1]
            high = d2[m] * below[m]
            to[c, m, pl.ds(rows, rows), :] = high if m == size - 1 else high + d3[m] * above[m + 1]
        for d in range(size - 1, 0, -1):
            t = other(d, d > 1)
            remote(to.at[c, t], ti.at[c, own], sent.at[0], r2.at[c], gx=group * size + t).start()
        ti[c, own, :] = to[c, rank]

    def gathered(system, side, by=1.0):
        def way(q, p):
            return 1 - side if q == p else (0 if q < p else 1)

        return [
            pick(wall, [by * system.weights[side, (p - d) % py, way((p - d) % py, p), p] for p in range(py)])
            for d in range(py)
        ]

    def side_of(systems, place, out):
        return [
            (
                pick(place, -out[s] * system.off * system.fix_low), pick(place, out[s] * system.edge_low),
                pick(place, -out[s] * system.off * system.fix_high), pick(place, out[s] * system.edge_high),
            )
            for s, system in enumerate(systems)
        ]

    near_y = side_of(sys_y, wall, OUT)
    outer_y = [[gathered(s, side, -OUT[k] * s.off) for side in range(2)] for k, s in enumerate(sys_y)]
    wide = WIDE

    def solve_y(index, _):
        c = index // (mx // wide)
        first_row = pl.multiple_of(lax.rem(index, mx // wide) * wide, wide)
        part = pl.ds(first_row, wide)
        cells = [jnp.where(wall > 0, yin[c, 0, 0, part, :], 0.0)]
        cells += [vt[c, y, part, :] for y in range(my)]
        cells += [jnp.where(wall < py - 1, yin[c, py - 2, 0, part, :], 0.0)]
        more = [
            [
                total(
                    [outer_y[s][side][0] * yout[c, 1 - side, 1 + s, part, :]]
                    + [outer_y[s][side][d] * yin[c, d - 1, 1 + s, part, :] for d in range(1, py)]
                    + [near_y[s][2 * side] * cells[0 - side], near_y[s][2 * side + 1] * cells[1 if side == 0 else my]]
                )
                for s in range(2)
            ]
            for side in range(2)
        ]
        for values, out in zip(line(sys_y, cells, *more), (fy, sy)):
            for i, value in enumerate(values):
                out[c, pl.ds(first_row * my + i, wide, stride=my), :] = value
        return 0

    near_x = side_of(sys_x, me, OUT)
    tile = 16 if my % 16 == 0 else 8

    def solve_x(index, _):
        c = index // (my // tile)
        start = pl.multiple_of(lax.rem(index, my // tile) * tile, tile)
        cells = [xlo[c, pl.ds(start, tile), :]]
        cells += [v[c, pl.ds(i * my + start, tile), :] for i in range(mx)]
        cells += [xhi[c, pl.ds(start, tile), :]]
        more = [
            [near_x[s][2 * side] * cells[0 - side] + near_x[s][2 * side + 1] * cells[1 if side == 0 else mx] for s in range(2)]
            for side in range(2)
        ]
        first, second = line(sys_x, cells, *more)
        for i in range(mx):
            part = pl.ds(i * my + start, tile)
            conv[c, part, :] = conv[c, part, :] + (v[0, part, :] * first[i] + v[1, part, :] * fy[c, part, :])
            expl[c, part, :] = expl[c, part, :] + (second[i] + sy[c, part, :])
        return 0

    for c in range(nc):
        exchange(c)
    for c in range(nc):
        solve_z(c)
    for c in range(nc):
        arrived(yin.at[c], yr.at[c])
    lax.fori_loop(0, nc * (mx // wide), solve_y, 0)

    @pl.when(me > 0)
    def _():
        up.wait_recv()

    @pl.when(me == 0)
    def _():
        xlo[...] = jnp.zeros_like(xlo)

    @pl.when(me < px - 1)
    def _():
        down.wait_recv()

    @pl.when(me == px - 1)
    def _():
        xhi[...] = jnp.zeros_like(xhi)

    lax.fori_loop(0, nc * (my // tile), solve_x, 0)

    def far(s, side, dg):
        values = []
        for p in range(px):
            g, q = p // size, (p // size - dg) % groups
            if q < g:
                value = s.d[p, 2 * side]
                for k in range((q + 1) * size, p + side):
                    value = value * s.t[k, 0]
            else:
                value = s.d[p, 2 * side + 1]
                for k in range(p + side, q * size):
                    value = value * s.t[k, 1]
            values.append(value)
        return pick(me, values)

    far_x = [[[far(s, side, dg) for dg in range(1, groups)] for side in range(2)] for s in sys_x]
    right_w = [pick(wall, sys_w.right[:, i]) for i in range(my)]
    left_w = [pick(wall, sys_w.left[:, i]) for i in range(my)]
    outer_w = [gathered(sys_w, side) for side in range(2)]
    back = 2 * rows * (size - 1) + (groups - 1) * 2 * my

    for c in range(nc):
        arrived(ti.at[c, pl.ds(0, back)], r2.at[c])
        outer = []
        for s in range(2):
            pair = []
            for side in range(2):
                value = jnp.concatenate(
                    [ti[c, pl.ds(b * 2 * rows + side * rows, rows), :] for b in range(s * half, (s + 1) * half)], axis=0
                )
                for dg in range(1, groups):
                    at = 4 * my + (dg - 1) * 2 * my + s * my
                    value = value + far_x[s][side][dg - 1] * ti[c, pl.ds(at, my), :]
                pair.append(value)
            outer.append(pair)
        for i in range(mx):
            part = pl.ds(i * my, my)
            more = sys_x[0].low[i] * outer[0][0] + sys_x[0].high[i] * outer[0][1]
            bend = (viscosity * sys_x[1].low[i]) * outer[1][0] + (viscosity * sys_x[1].high[i]) * outer[1][1]
            moved = conv[c, part, :] + v[0, part, :] * more
            conv[c, part, :] = moved
            expl[c, part, :] = expl[c, part, :] + (bend - (time_step * gamma_now) * moved)
        low = high = None
        for i in range(my):
            row = yrow(expl, c, i)
            et[c, i] = row
            low = right_w[i] * row if low is None else low + right_w[i] * row
            high = left_w[i] * row if high is None else high + left_w[i] * row
        gw[c, 0] = low
        gw[c, 1] = high
        for d in range(1, py):
            peer = lax.rem(wall + d, py)
            way = jnp.where(peer > wall, 0, 1)
            remote(gw.at[c, way], gwr.at[c, d - 1], sent.at[0], wr.at[c], gy=peer).start()

    def solve_w(c, _):
        for i, value in enumerate(sys_w.solve([et[c, y] for y in range(my)])):
            base[c, pl.ds(i, mx, stride=my), :] = value
        return 0

    lax.fori_loop(0, nc, solve_w, 0)
    for c in range(nc):
        arrived(gwr.at[c], wr.at[c])
        for side in range(2):
            ends_w[c, side] = total(
                [outer_w[side][0] * gw[c, 1 - side]]
                + [outer_w[side][d] * gwr[c, d - 1] for d in range(1, py)]
            )

    arrived(tally, sent.at[0])
    arrived(v, sent.at[1])

    @pl.when(me < px - 1)
    def _():
        up.wait_send()

    @pl.when(me > 0)
    def _():
        down.wait_send()


def finish(cfg, conv_in, base, ends_w, shape_w, conv, upd, built, sem):
    nc, mx, my = cfg
    writes = [pltpu.make_async_copy(conv_in.at[c], conv.at[c], sem.at[c]) for c in range(nc)]
    for write in writes:
        write.start()
    for c in range(nc):
        for i in range(mx):
            part = pl.ds(i * my, my)
            built[c, part, :] = base[c, part, :] + (
                shape_w[0] * ends_w[c, 0, pl.ds(i, 1), :] + shape_w[1] * ends_w[c, 1, pl.ds(i, 1), :]
            )
        write = pltpu.make_async_copy(built.at[c], upd.at[c], sem.at[nc + c])
        write.start()
        writes.append(write)
    for write in writes:
        write.wait()


def body(counts, velocity, conv_prev):
    px, py, pz = counts
    nc, mx, my, nz = velocity.shape
    size = 4 if px % 4 == 0 else 2
    groups = px // size
    rows = 2 * my // size
    assert pz == 2 and py > 1 and px % 2 == 0 and rows % 8 == 0 and mx % 8 == 0
    flat = (nc, mx * my, nz)
    f32 = jnp.float32
    sent = 2 * rows * (size - 1) * 2 + (groups - 1) * size * rows + (py - 1) * 4 * mx

    def vmem(*shape):
        return pltpu.VMEM(shape, f32)

    def dma(n):
        return pltpu.SemaphoreType.DMA((n,))

    def out(*shape):
        return jax.ShapeDtypeStruct(shape, f32)

    whole = pl.BlockSpec(memory_space=pltpu.VMEM)
    velocity = pltpu.with_memory_space_constraint(velocity.reshape(flat), pltpu.HBM)
    conv_prev = pltpu.with_memory_space_constraint(conv_prev.reshape(flat), pltpu.HBM)
    hbm = pl.BlockSpec(memory_space=pltpu.HBM)
    parts = pl.pallas_call(
        functools.partial(kernel, (nc, mx, my, nz, px, py, size, groups)),
        out_shape=[out(*flat), out(*flat), out(nc, 2, mx, nz), out(2, my, nz)],
        in_specs=[hbm, hbm],
        out_specs=[whole] * 4,
        scratch_shapes=[
            vmem(*flat), vmem(*flat), vmem(*flat),
            vmem(nc, my, nz), vmem(nc, my, nz),
            vmem(nc, 4 * my, nz), vmem(nc, size, 2 * rows, nz), vmem(nc, size, 2 * rows, nz),
            vmem(nc, 2, rows, nz), vmem(nc, 4 * my + (groups - 1) * 2 * my, nz),
            vmem(nc, 2, 3, mx, nz), vmem(nc, py - 1, 3, mx, nz),
            vmem(nc, my, mx, nz), vmem(*flat), vmem(*flat), vmem(*flat), vmem(nc, my, mx, nz),
            vmem(nc, 2, mx, nz), vmem(nc, py - 1, mx, nz), vmem(nc * sent, nz),
            dma(nc + 1), dma(nc), dma(nc), dma(nc), dma(nc), dma(nc), dma(2), dma(2), dma(2),
        ],
        compiler_params=pltpu.CompilerParams(
            collective_id=0, has_side_effects=True, vmem_limit_bytes=32 * 1024 * 1024
        ),
    )(velocity, conv_prev)
    conv, upd = pl.pallas_call(
        functools.partial(finish, (nc, mx, my)),
        out_shape=[out(*flat), out(*flat)],
        in_specs=[whole] * 4,
        out_specs=[hbm, hbm],
        scratch_shapes=[vmem(*flat), dma(2 * nc)],
        compiler_params=pltpu.CompilerParams(vmem_limit_bytes=16 * 1024 * 1024),
    )(*parts)
    return conv.reshape(nc, mx, my, nz), upd.reshape(nc, mx, my, nz)


def solution(mesh):
    spec = P(None, "gx", "gy", "gz")
    counts = tuple(mesh.shape[name] for name in ("gx", "gy", "gz"))
    return jax.shard_map(
        functools.partial(body, counts), mesh=mesh, in_specs=(spec, spec),
        out_specs=(spec, spec), check_vma=False,
    )
```

```python
import collections
import functools

import jax
import jax.numpy as jnp
import numpy as np
from jax import lax
from jax.experimental import pallas as pl
from jax.experimental.pallas import tpu as pltpu
from jax.sharding import PartitionSpec as P

MESH = pl.DeviceIdType.MESH
WIDE = 8
time_step = 1.0
gamma_now = 5.0 / 12.0
zeta_old = -17.0 / 60.0
viscosity = 0.1

OFF = (1.0 / 3.0, 2.0 / 11.0)
EDGE = (1.0 / 36.0, 3.0 / 44.0)
NEAR = (EDGE[0] / OFF[0], EDGE[1] / OFF[1])
MID = (12.0 / 11.0 - NEAR[1]) / OFF[1]
REST = (7.0 / 9.0 - NEAR[0], -24.0 / 11.0 - 4.0 * EDGE[1] - MID)
COMPACT = (
    (OFF[0], 1.0, {1: REST[0], -1: -REST[0]}, (EDGE[0], -EDGE[0])),
    (OFF[1], 1.0, {0: REST[1]}, (EDGE[1], EDGE[1])),
)
OUT = (1.0, viscosity)


class System:
    def __init__(self, off, mid, stencil, edges, count, m):
        n = count * m
        rho = np.zeros(n + 2)
        last = 0.0
        for j in range(n + 2):
            last = -off / (mid + off * last)
            rho[j] = last

        def u(j, ref):
            if j < 0:
                return 0.0
            if j <= ref:
                return float(np.prod(rho[j:ref]))
            return 1.0 / float(np.prod(rho[ref:j]))

        def v(j, ref):
            return u(n - 1 - j, n - 1 - ref)

        def inv(i, j):
            low = rho[i - 1] if i > 0 else 0.0
            high = rho[n - 2 - i] if i < n - 1 else 0.0
            diag = 1.0 / (mid + off * low + off * high)
            return diag * (u(j, i) if j <= i else v(j, i))

        def b(j, col):
            extra = edges[0] if j == col == 0 else edges[1] if j == col == n - 1 else 0.0
            return stencil.get(col - j, 0.0) + extra

        self.off, self.m, self.count = off, m, count
        self.right, self.left = np.zeros((count, m)), np.zeros((count, m))
        self.fix_low, self.fix_high = np.zeros(count), np.zeros(count)
        self.edge_low, self.edge_high = np.zeros(count), np.zeros(count)
        self.edge_low[0], self.edge_high[-1] = edges
        self.d = np.zeros((count, 4))
        self.t = np.zeros((count, 2))
        self.weights = np.zeros((2, count, 2, count))
        for p in range(count):
            start, end = p * m, p * m + m - 1
            for k in range(m):
                col = start + k
                rows = [j for j in range(col - 2, col + 3) if 0 <= j < n]
                self.right[p, k] = sum(u(j, end) * b(j, col) for j in rows)
                self.left[p, k] = sum(v(j, start) * b(j, col) for j in rows)
            if p > 0:
                e = start - 1
                self.fix_low[p] = (inv(e, e + 1) - inv(e, e) * u(e + 1, e)) * b(e + 1, e)
                self.d[p, 0], self.d[p, 1] = inv(e, e), inv(e, e + 1)
                self.t[p, 0] = u(e, end)
                for q in range(count):
                    if q < p:
                        self.weights[0, q, 0, p] = inv(e, q * m + m - 1)
                    else:
                        self.weights[0, q, 1, p] = inv(e, q * m)
            if p < count - 1:
                f = end + 1
                self.fix_high[p] = (inv(f, f - 1) - inv(f, f) * v(f - 1, f)) * b(f - 1, f)
                self.d[p, 2], self.d[p, 3] = inv(f, f - 1), inv(f, f)
                self.t[p, 1] = v(f, start)
                for q in range(count):
                    if q > p:
                        self.weights[1, q, 1, p] = inv(f, q * m)
                    else:
                        self.weights[1, q, 0, p] = inv(f, q * m + m - 1)
        pivots, ratios, last = [], [], 0.0
        for _ in range(m):
            pivot = mid - off * last
            last = off / pivot
            pivots.append(pivot)
            ratios.append(last)
        self.scale = [float(1.0 / pivot) for pivot in pivots]
        self.ratio = [float(ratio) for ratio in ratios]
        unit = np.zeros(m)
        unit[0] = 1.0
        self.low = [-off * value for value in self.solve(list(unit))]
        self.high = self.low[::-1]

    def solve(self, rows):
        return self.sweep([row * self.scale[i] for i, row in enumerate(rows)])

    def sweep(self, scaled):
        done, carry = [], None
        for i, fresh in enumerate(scaled):
            carry = fresh if carry is None else fresh - self.ratio[i] * carry
            done.append(carry)
        for i in range(self.m - 2, -1, -1):
            done[i] = done[i] - self.ratio[i] * done[i + 1]
        return done


def pick(place, values):
    values = [float(np.float32(value)) for value in values]
    common = collections.Counter(values).most_common(1)[0][0]
    result = jnp.float32(common)
    for index, value in enumerate(values):
        if value != common:
            result = jnp.where(place == index, jnp.float32(value), result)
    return result


def line(systems, cells, low, high):
    m = len(cells) - 2
    odd = [cells[i + 2] - cells[i] for i in range(m)]
    even = [cells[i + 2] + cells[i] for i in range(m)]
    solved = []
    for s in range(2):
        system = systems[s]
        source = odd if s == 0 else cells[1:-1]
        scaled = [(REST[s] * OUT[s] * system.scale[i]) * source[i] for i in range(m)]
        scaled[0] = scaled[0] + low[s] * system.scale[0]
        scaled[m - 1] = scaled[m - 1] + high[s] * system.scale[m - 1]
        solved.append(system.sweep(scaled))
    first = [solved[0][i] + NEAR[0] * odd[i] for i in range(m)]
    second = [
        solved[1][i] + ((NEAR[1] * viscosity) * even[i] + (MID * viscosity) * cells[i + 1]) for i in range(m)
    ]
    return first, second


def total(terms):
    return functools.reduce(lambda a, b: a + b, terms)


def kernel(
    cfg, v_hbm, cp_hbm, conv, base, ends_w, shape_w,
    v, cp, zo, xlo, xhi, gx, gr, to, st, ti, yout, yin, vt, fy, sy, expl, et, gw, gwr, tally,
    load, r1, r2, yr, zr, wr, hs, hr, sent,
):
    nc, mx, my, nz, px, py, size, groups = cfg
    rows = 2 * my // size
    me = lax.axis_index("gx")
    wall = lax.axis_index("gy")
    core = lax.axis_index("gz")
    group, rank = me // size, lax.rem(me, size)
    sys_x = [System(*pair, px, mx) for pair in COMPACT]
    sys_y = [System(*pair, py, my) for pair in COMPACT]
    beta = 4.0 * my * my
    sys_w = System(-beta, 1.0 + 2.0 * beta, {0: 1.0}, (0.0, 0.0), py, my)

    barrier = pltpu.get_barrier_semaphore()

    def greet(**device):
        pl.semaphore_signal(barrier, inc=1, device_id=device, device_id_type=MESH)

    for d in range(1, size):
        greet(gx=group * size + lax.rem(rank + d, size))
    for d in range(1, groups):
        greet(gx=lax.rem(group + d, groups) * size + rank)
    for d in range(1, py):
        greet(gy=lax.rem(wall + d, py))
    greet(gz=1 - core)
    is_last = (rank == size - 1) & (me < px - 1)
    is_first = (rank == 0) & (me > 0)

    @pl.when(is_last)
    def _():
        greet(gx=me + 1)

    @pl.when(is_first)
    def _():
        greet(gx=me - 1)

    reads = [pltpu.make_async_copy(v_hbm.at[c], v.at[c], load.at[c]) for c in range(nc)]
    reads.append(pltpu.make_async_copy(cp_hbm, cp, load.at[nc]))
    for read in reads:
        read.start()

    def remote(src, dst, send, recv, **target):
        return pltpu.make_async_remote_copy(
            src_ref=src, dst_ref=dst, send_sem=send, recv_sem=recv,
            device_id=target, device_id_type=MESH,
        )

    def arrived(ref, sem):
        pltpu.make_async_copy(ref, ref, sem).wait()

    def other(d, flip=False):
        if size & (size - 1):
            return lax.rem(rank + d, size)
        result, bit = 0, 1
        while bit < size:
            mine = lax.rem(rank // bit, 2)
            if bit == 1 and flip:
                mine = lax.rem(mine + core, 2)
            result = result + bit * ((1 - mine) if d & bit else mine)
            bit *= 2
        return result

    weigh_x = [
        [[pick(me, table[:, i]) for i in range(mx)] for table in (s.right, s.left)] for s in sys_x
    ]

    def sums_x(c):
        def step(b, _):
            part = [v[c, pl.ds(pl.multiple_of(i * my + b * 8, 8), 8), :] for i in range(mx)]
            for s in range(2):
                for way in range(2):
                    value = total([weigh_x[s][way][i] * part[i] for i in range(mx)])
                    flat = s * my + b * 8
                    owner = flat // rows
                    at = owner * 2 * rows + way * rows + lax.rem(flat, rows)
                    gx[c, pl.ds(pl.multiple_of(at, 8), 8), :] = value
            return 0

        lax.fori_loop(0, my // 8, step, 0)

    own = pl.ds(pl.multiple_of(rank * 2 * rows, 8), 2 * rows)
    for c in range(nc):
        reads[c].wait()
        sums_x(c)
        if c == 0:
            pl.semaphore_wait(
                barrier, size - 1 + groups - 1 + py - 1 + 1 + jnp.where(is_last | is_first, 1, 0)
            )
        for d in range(size - 1, 0, -1):
            t = other(d, d > 1)
            remote(
                gx.at[c, pl.ds(pl.multiple_of(t * 2 * rows, 8), 2 * rows)], gr.at[c, rank],
                sent.at[0], r1.at[c], gx=group * size + t,
            ).start()
        gr[c, rank] = gx[c, own, :]

    for c in range(nc):
        remote(v.at[c], zo.at[c], sent.at[1], zr.at[c], gz=1 - core).start()
    up = remote(v.at[:, pl.ds((mx - 1) * my, my)], xlo, hs.at[0], hr.at[0], gx=lax.rem(me + 1, px))
    down = remote(v.at[:, pl.ds(0, my)], xhi, hs.at[1], hr.at[1], gx=lax.rem(me + px - 1, px))

    @pl.when((me < px - 1) & (core == 0))
    def _():
        up.start()

    @pl.when((me > 0) & (core == 0))
    def _():
        down.start()

    def yrow(ref, c, y):
        return ref[c, pl.ds(y, mx, stride=my), :]

    weigh_y = [
        [[pick(wall, table[:, i]) for i in range(my)] for table in (s.right, s.left)] for s in sys_y
    ]

    def sums_y(c, _):
        sums = [[None, None], [None, None]]
        for i in range(my):
            row = yrow(v, c, i)
            vt[c, i] = row
            if i == 0:
                yout[c, 1, 0] = row
            if i == my - 1:
                yout[c, 0, 0] = row
            for s in range(2):
                for way in range(2):
                    term = weigh_y[s][way][i] * row
                    sums[s][way] = term if i == 0 else sums[s][way] + term
        for s in range(2):
            for way in range(2):
                yout[c, way, 1 + s] = sums[s][way]
        for d in range(1, py):
            peer = lax.rem(wall + d, py)
            way = jnp.where(peer > wall, 0, 1)
            remote(yout.at[c, way], yin.at[c, d - 1], sent.at[0], yr.at[c], gy=peer).start()
        return 0

    for c in range(nc):
        sums_y(c, 0)

    for i in range(my):
        shape_w[0, pl.ds(i, 1), :] = jnp.full((1, nz), sys_w.low[i], jnp.float32)
        shape_w[1, pl.ds(i, 1), :] = jnp.full((1, nz), sys_w.high[i], jnp.float32)

    slab = mx * my
    lane = lax.broadcasted_iota(jnp.int32, (slab, nz), 1)
    reads[nc].wait()

    def solve_z(c):
        def step(index, _):
            part = pl.ds(pl.multiple_of(index * slab, slab), slab)
            mine, rest = v[c, part, :], zo[c, part, :]

            def after(k):
                return pltpu.roll(jnp.where(lane < k, rest, mine), nz - k, 1)

            def before(k):
                return pltpu.roll(jnp.where(lane >= nz - k, rest, mine), k, 1)

            high, low = [after(k) for k in (1, 2, 3)], [before(k) for k in (1, 2, 3)]
            odd = [a - b for a, b in zip(high, low)]
            even = [a + b for a, b in zip(high, low)]
            first = (45.0 / 60.0) * odd[0] - (9.0 / 60.0) * odd[1] + (1.0 / 60.0) * odd[2]
            bend = (
                (viscosity * 2.0 / 180.0) * even[2] - (viscosity * 27.0 / 180.0) * even[1]
                + (viscosity * 270.0 / 180.0) * even[0] + (1.0 - viscosity * 490.0 / 180.0) * mine
            )
            conv[c, part, :] = v[2, part, :] * first
            expl[c, part, :] = bend - (time_step * zeta_old) * cp[c, part, :]
            return 0

        arrived(zo.at[c], zr.at[c])
        lax.fori_loop(0, mx * my // slab, step, 0)

    half = size // 2
    share = rank // half

    def table(field):
        return [
            pick(group * 2 + share, [field(sys_x[s], g * size + m) for g in range(groups) for s in range(2)])
            for m in range(size)
        ]

    t0, t1 = (table(lambda s, p, k=k: s.t[p, k]) for k in range(2))
    d0, d1, d2, d3 = (table(lambda s, p, k=k: s.d[p, k]) for k in range(4))

    def exchange(c):
        arrived(gr.at[c, pl.ds(0, size - 1)], r1.at[c])
        below, above = [None] * size, [None] * size
        for m in range(size):
            here = gr[c, m, pl.ds(0, rows), :]
            below[m] = here if m == 0 else here + t0[m] * below[m - 1]
        for m in reversed(range(size)):
            here = gr[c, m, pl.ds(rows, rows), :]
            above[m] = here if m == size - 1 else here + t1[m] * above[m + 1]
        if groups > 1:
            st[c, 0] = below[size - 1]
            st[c, 1] = above[0]
            for dg in range(1, groups):
                there = lax.rem(group + dg, groups)
                way = jnp.where(there > group, 0, 1)
                at = pl.multiple_of(4 * my + (dg - 1) * 2 * my + rank * rows, 8)
                for d in range(size - 1, -1, -1):
                    m = other(d, True)
                    remote(
                        st.at[c, way], ti.at[c, pl.ds(at, rows)], sent.at[0], r2.at[c],
                        gx=there * size + m,
                    ).start()
        for m in range(size):
            low = d1[m] * above[m]
            to[c, m, pl.ds(0, rows), :] = low if m == 0 else low + d0[m] * below[m - 1]
            high = d2[m] * below[m]
            to[c, m, pl.ds(rows, rows), :] = high if m == size - 1 else high + d3[m] * above[m + 1]
        for d in range(size - 1, 0, -1):
            t = other(d, d > 1)
            remote(to.at[c, t], ti.at[c, own], sent.at[0], r2.at[c], gx=group * size + t).start()
        ti[c, own, :] = to[c, rank]

    def gathered(system, side, by=1.0):
        def way(q, p):
            return 1 - side if q == p else (0 if q < p else 1)

        return [
            pick(wall, [by * system.weights[side, (p - d) % py, way((p - d) % py, p), p] for p in range(py)])
            for d in range(py)
        ]

    def side_of(systems, place, out):
        return [
            (
                pick(place, -out[s] * system.off * system.fix_low), pick(place, out[s] * system.edge_low),
                pick(place, -out[s] * system.off * system.fix_high), pick(place, out[s] * system.edge_high),
            )
            for s, system in enumerate(systems)
        ]

    near_y = side_of(sys_y, wall, OUT)
    outer_y = [[gathered(s, side, -OUT[k] * s.off) for side in range(2)] for k, s in enumerate(sys_y)]
    wide = WIDE

    def solve_y(index, _):
        c = index // (mx // wide)
        first_row = pl.multiple_of(lax.rem(index, mx // wide) * wide, wide)
        part = pl.ds(first_row, wide)
        cells = [jnp.where(wall > 0, yin[c, 0, 0, part, :], 0.0)]
        cells += [vt[c, y, part, :] for y in range(my)]
        cells += [jnp.where(wall < py - 1, yin[c, py - 2, 0, part, :], 0.0)]
        more = [
            [
                total(
                    [outer_y[s][side][0] * yout[c, 1 - side, 1 + s, part, :]]
                    + [outer_y[s][side][d] * yin[c, d - 1, 1 + s, part, :] for d in range(1, py)]
                    + [near_y[s][2 * side] * cells[0 - side], near_y[s][2 * side + 1] * cells[1 if side == 0 else my]]
                )
                for s in range(2)
            ]
            for side in range(2)
        ]
        for values, out in zip(line(sys_y, cells, *more), (fy, sy)):
            for i, value in enumerate(values):
                out[c, pl.ds(first_row * my + i, wide, stride=my), :] = value
        return 0

    near_x = side_of(sys_x, me, OUT)
    tile = 16 if my % 16 == 0 else 8

    def solve_x(index, _):
        c = index // (my // tile)
        start = pl.multiple_of(lax.rem(index, my // tile) * tile, tile)
        cells = [xlo[c, pl.ds(start, tile), :]]
        cells += [v[c, pl.ds(i * my + start, tile), :] for i in range(mx)]
        cells += [xhi[c, pl.ds(start, tile), :]]
        more = [
            [near_x[s][2 * side] * cells[0 - side] + near_x[s][2 * side + 1] * cells[1 if side == 0 else mx] for s in range(2)]
            for side in range(2)
        ]
        first, second = line(sys_x, cells, *more)
        for i in range(mx):
            part = pl.ds(i * my + start, tile)
            conv[c, part, :] = conv[c, part, :] + (v[0, part, :] * first[i] + v[1, part, :] * fy[c, part, :])
            expl[c, part, :] = expl[c, part, :] + (second[i] + sy[c, part, :])
        return 0

    for c in range(nc):
        exchange(c)

    @pl.when((me < px - 1) & (core == 1))
    def _():
        up.start()

    @pl.when((me > 0) & (core == 1))
    def _():
        down.start()

    for c in range(nc):
        solve_z(c)
    for c in range(nc):
        arrived(yin.at[c], yr.at[c])
    lax.fori_loop(0, nc * (mx // wide), solve_y, 0)

    @pl.when(me > 0)
    def _():
        up.wait_recv()

    @pl.when(me == 0)
    def _():
        xlo[...] = jnp.zeros_like(xlo)

    @pl.when(me < px - 1)
    def _():
        down.wait_recv()

    @pl.when(me == px - 1)
    def _():
        xhi[...] = jnp.zeros_like(xhi)

    lax.fori_loop(0, nc * (my // tile), solve_x, 0)

    def far(s, side, dg):
        values = []
        for p in range(px):
            g, q = p // size, (p // size - dg) % groups
            if q < g:
                value = s.d[p, 2 * side]
                for k in range((q + 1) * size, p + side):
                    value = value * s.t[k, 0]
            else:
                value = s.d[p, 2 * side + 1]
                for k in range(p + side, q * size):
                    value = value * s.t[k, 1]
            values.append(value)
        return pick(me, values)

    far_x = [[[far(s, side, dg) for dg in range(1, groups)] for side in range(2)] for s in sys_x]
    right_w = [pick(wall, sys_w.right[:, i]) for i in range(my)]
    left_w = [pick(wall, sys_w.left[:, i]) for i in range(my)]
    outer_w = [gathered(sys_w, side) for side in range(2)]
    back = 2 * rows * (size - 1) + (groups - 1) * 2 * my

    for c in range(nc):
        arrived(ti.at[c, pl.ds(0, back)], r2.at[c])
        outer = []
        for s in range(2):
            pair = []
            for side in range(2):
                value = jnp.concatenate(
                    [ti[c, pl.ds(b * 2 * rows + side * rows, rows), :] for b in range(s * half, (s + 1) * half)], axis=0
                )
                for dg in range(1, groups):
                    at = 4 * my + (dg - 1) * 2 * my + s * my
                    value = value + far_x[s][side][dg - 1] * ti[c, pl.ds(at, my), :]
                pair.append(value)
            outer.append(pair)
        for i in range(mx):
            part = pl.ds(i * my, my)
            more = sys_x[0].low[i] * outer[0][0] + sys_x[0].high[i] * outer[0][1]
            bend = (viscosity * sys_x[1].low[i]) * outer[1][0] + (viscosity * sys_x[1].high[i]) * outer[1][1]
            moved = conv[c, part, :] + v[0, part, :] * more
            conv[c, part, :] = moved
            expl[c, part, :] = expl[c, part, :] + (bend - (time_step * gamma_now) * moved)
        low = high = None
        for i in range(my):
            row = yrow(expl, c, i)
            et[c, i] = row
            low = right_w[i] * row if low is None else low + right_w[i] * row
            high = left_w[i] * row if high is None else high + left_w[i] * row
        gw[c, 0] = low
        gw[c, 1] = high
        for d in range(1, py):
            peer = lax.rem(wall + d, py)
            way = jnp.where(peer > wall, 0, 1)
            remote(gw.at[c, way], gwr.at[c, d - 1], sent.at[0], wr.at[c], gy=peer).start()

    def solve_w(c, _):
        for i, value in enumerate(sys_w.solve([et[c, y] for y in range(my)])):
            base[c, pl.ds(i, mx, stride=my), :] = value
        return 0

    lax.fori_loop(0, nc, solve_w, 0)
    for c in range(nc):
        arrived(gwr.at[c], wr.at[c])
        for side in range(2):
            ends_w[c, side] = total(
                [outer_w[side][0] * gw[c, 1 - side]]
                + [outer_w[side][d] * gwr[c, d - 1] for d in range(1, py)]
            )

    arrived(tally, sent.at[0])
    arrived(v, sent.at[1])

    @pl.when(me < px - 1)
    def _():
        up.wait_send()

    @pl.when(me > 0)
    def _():
        down.wait_send()


def finish(cfg, conv_in, base, ends_w, shape_w, conv, upd, built, sem):
    nc, mx, my = cfg
    writes = [pltpu.make_async_copy(conv_in.at[c], conv.at[c], sem.at[c]) for c in range(nc)]
    for write in writes:
        write.start()
    for c in range(nc):
        for i in range(mx):
            part = pl.ds(i * my, my)
            built[c, part, :] = base[c, part, :] + (
                shape_w[0] * ends_w[c, 0, pl.ds(i, 1), :] + shape_w[1] * ends_w[c, 1, pl.ds(i, 1), :]
            )
        write = pltpu.make_async_copy(built.at[c], upd.at[c], sem.at[nc + c])
        write.start()
        writes.append(write)
    for write in writes:
        write.wait()


def body(counts, velocity, conv_prev):
    px, py, pz = counts
    nc, mx, my, nz = velocity.shape
    size = 4 if px % 4 == 0 else 2
    groups = px // size
    rows = 2 * my // size
    assert pz == 2 and py > 1 and px % 2 == 0 and rows % 8 == 0 and mx % 8 == 0
    flat = (nc, mx * my, nz)
    f32 = jnp.float32
    sent = 2 * rows * (size - 1) * 2 + (groups - 1) * size * rows + (py - 1) * 4 * mx

    def vmem(*shape):
        return pltpu.VMEM(shape, f32)

    def dma(n):
        return pltpu.SemaphoreType.DMA((n,))

    def out(*shape):
        return jax.ShapeDtypeStruct(shape, f32)

    whole = pl.BlockSpec(memory_space=pltpu.VMEM)
    velocity = pltpu.with_memory_space_constraint(velocity.reshape(flat), pltpu.HBM)
    conv_prev = pltpu.with_memory_space_constraint(conv_prev.reshape(flat), pltpu.HBM)
    hbm = pl.BlockSpec(memory_space=pltpu.HBM)
    parts = pl.pallas_call(
        functools.partial(kernel, (nc, mx, my, nz, px, py, size, groups)),
        out_shape=[out(*flat), out(*flat), out(nc, 2, mx, nz), out(2, my, nz)],
        in_specs=[hbm, hbm],
        out_specs=[whole] * 4,
        scratch_shapes=[
            vmem(*flat), vmem(*flat), vmem(*flat),
            vmem(nc, my, nz), vmem(nc, my, nz),
            vmem(nc, 4 * my, nz), vmem(nc, size, 2 * rows, nz), vmem(nc, size, 2 * rows, nz),
            vmem(nc, 2, rows, nz), vmem(nc, 4 * my + (groups - 1) * 2 * my, nz),
            vmem(nc, 2, 3, mx, nz), vmem(nc, py - 1, 3, mx, nz),
            vmem(nc, my, mx, nz), vmem(*flat), vmem(*flat), vmem(*flat), vmem(nc, my, mx, nz),
            vmem(nc, 2, mx, nz), vmem(nc, py - 1, mx, nz), vmem(nc * sent, nz),
            dma(nc + 1), dma(nc), dma(nc), dma(nc), dma(nc), dma(nc), dma(2), dma(2), dma(2),
        ],
        compiler_params=pltpu.CompilerParams(
            collective_id=0, has_side_effects=True, vmem_limit_bytes=32 * 1024 * 1024
        ),
    )(velocity, conv_prev)
    conv, upd = pl.pallas_call(
        functools.partial(finish, (nc, mx, my)),
        out_shape=[out(*flat), out(*flat)],
        in_specs=[whole] * 4,
        out_specs=[hbm, hbm],
        scratch_shapes=[vmem(*flat), dma(2 * nc)],
        compiler_params=pltpu.CompilerParams(vmem_limit_bytes=16 * 1024 * 1024),
    )(*parts)
    return conv.reshape(nc, mx, my, nz), upd.reshape(nc, mx, my, nz)


def solution(mesh):
    spec = P(None, "gx", "gy", "gz")
    counts = tuple(mesh.shape[name] for name in ("gx", "gy", "gz"))
    return jax.shard_map(
        functools.partial(body, counts), mesh=mesh, in_specs=(spec, spec),
        out_specs=(spec, spec), check_vma=False,
    )
```

```python
import collections
import functools

import jax
import jax.numpy as jnp
import numpy as np
from jax import lax
from jax.experimental import pallas as pl
from jax.experimental.pallas import tpu as pltpu
from jax.sharding import PartitionSpec as P

MESH = pl.DeviceIdType.MESH
WIDE = 8
time_step = 1.0
gamma_now = 5.0 / 12.0
zeta_old = -17.0 / 60.0
viscosity = 0.1

OFF = (1.0 / 3.0, 2.0 / 11.0)
EDGE = (1.0 / 36.0, 3.0 / 44.0)
NEAR = (EDGE[0] / OFF[0], EDGE[1] / OFF[1])
MID = (12.0 / 11.0 - NEAR[1]) / OFF[1]
REST = (7.0 / 9.0 - NEAR[0], -24.0 / 11.0 - 4.0 * EDGE[1] - MID)
COMPACT = (
    (OFF[0], 1.0, {1: REST[0], -1: -REST[0]}, (EDGE[0], -EDGE[0])),
    (OFF[1], 1.0, {0: REST[1]}, (EDGE[1], EDGE[1])),
)
OUT = (1.0, viscosity)


class System:
    def __init__(self, off, mid, stencil, edges, count, m):
        n = count * m
        rho = np.zeros(n + 2)
        last = 0.0
        for j in range(n + 2):
            last = -off / (mid + off * last)
            rho[j] = last

        def u(j, ref):
            if j < 0:
                return 0.0
            if j <= ref:
                return float(np.prod(rho[j:ref]))
            return 1.0 / float(np.prod(rho[ref:j]))

        def v(j, ref):
            return u(n - 1 - j, n - 1 - ref)

        def inv(i, j):
            low = rho[i - 1] if i > 0 else 0.0
            high = rho[n - 2 - i] if i < n - 1 else 0.0
            diag = 1.0 / (mid + off * low + off * high)
            return diag * (u(j, i) if j <= i else v(j, i))

        def b(j, col):
            extra = edges[0] if j == col == 0 else edges[1] if j == col == n - 1 else 0.0
            return stencil.get(col - j, 0.0) + extra

        self.off, self.m, self.count = off, m, count
        self.right, self.left = np.zeros((count, m)), np.zeros((count, m))
        self.fix_low, self.fix_high = np.zeros(count), np.zeros(count)
        self.edge_low, self.edge_high = np.zeros(count), np.zeros(count)
        self.edge_low[0], self.edge_high[-1] = edges
        self.d = np.zeros((count, 4))
        self.t = np.zeros((count, 2))
        self.weights = np.zeros((2, count, 2, count))
        for p in range(count):
            start, end = p * m, p * m + m - 1
            for k in range(m):
                col = start + k
                rows = [j for j in range(col - 2, col + 3) if 0 <= j < n]
                self.right[p, k] = sum(u(j, end) * b(j, col) for j in rows)
                self.left[p, k] = sum(v(j, start) * b(j, col) for j in rows)
            if p > 0:
                e = start - 1
                self.fix_low[p] = (inv(e, e + 1) - inv(e, e) * u(e + 1, e)) * b(e + 1, e)
                self.d[p, 0], self.d[p, 1] = inv(e, e), inv(e, e + 1)
                self.t[p, 0] = u(e, end)
                for q in range(count):
                    if q < p:
                        self.weights[0, q, 0, p] = inv(e, q * m + m - 1)
                    else:
                        self.weights[0, q, 1, p] = inv(e, q * m)
            if p < count - 1:
                f = end + 1
                self.fix_high[p] = (inv(f, f - 1) - inv(f, f) * v(f - 1, f)) * b(f - 1, f)
                self.d[p, 2], self.d[p, 3] = inv(f, f - 1), inv(f, f)
                self.t[p, 1] = v(f, start)
                for q in range(count):
                    if q > p:
                        self.weights[1, q, 1, p] = inv(f, q * m)
                    else:
                        self.weights[1, q, 0, p] = inv(f, q * m + m - 1)
        pivots, ratios, last = [], [], 0.0
        for _ in range(m):
            pivot = mid - off * last
            last = off / pivot
            pivots.append(pivot)
            ratios.append(last)
        self.scale = [float(1.0 / pivot) for pivot in pivots]
        self.ratio = [float(ratio) for ratio in ratios]
        unit = np.zeros(m)
        unit[0] = 1.0
        self.low = [-off * value for value in self.solve(list(unit))]
        self.high = self.low[::-1]

    def solve(self, rows):
        return self.sweep([row * self.scale[i] for i, row in enumerate(rows)])

    def sweep(self, scaled):
        done, carry = [], None
        for i, fresh in enumerate(scaled):
            carry = fresh if carry is None else fresh - self.ratio[i] * carry
            done.append(carry)
        for i in range(self.m - 2, -1, -1):
            done[i] = done[i] - self.ratio[i] * done[i + 1]
        return done


def pick(place, values):
    values = [float(np.float32(value)) for value in values]
    common = collections.Counter(values).most_common(1)[0][0]
    result = jnp.float32(common)
    for index, value in enumerate(values):
        if value != common:
            result = jnp.where(place == index, jnp.float32(value), result)
    return result


def line(systems, cells, low, high):
    m = len(cells) - 2
    odd = [cells[i + 2] - cells[i] for i in range(m)]
    even = [cells[i + 2] + cells[i] for i in range(m)]
    solved = []
    for s in range(2):
        system = systems[s]
        source = odd if s == 0 else cells[1:-1]
        scaled = [(REST[s] * OUT[s] * system.scale[i]) * source[i] for i in range(m)]
        scaled[0] = scaled[0] + low[s] * system.scale[0]
        scaled[m - 1] = scaled[m - 1] + high[s] * system.scale[m - 1]
        solved.append(system.sweep(scaled))
    first = [solved[0][i] + NEAR[0] * odd[i] for i in range(m)]
    second = [
        solved[1][i] + ((NEAR[1] * viscosity) * even[i] + (MID * viscosity) * cells[i + 1]) for i in range(m)
    ]
    return first, second


def total(terms):
    return functools.reduce(lambda a, b: a + b, terms)


def kernel(
    cfg, v_hbm, cp_hbm, conv, base, ends_w, shape_w,
    v, cp, zo, xlo, xhi, gx, gr, to, st, ti, yout, yin, vt, fy, sy, expl, et, gw, gwr, tally,
    load, r1, r2, yr, zr, wr, hs, hr, sent,
):
    nc, mx, my, nz, px, py, size, groups = cfg
    rows = 2 * my // size
    me = lax.axis_index("gx")
    wall = lax.axis_index("gy")
    core = lax.axis_index("gz")
    group, rank = me // size, lax.rem(me, size)
    sys_x = [System(*pair, px, mx) for pair in COMPACT]
    sys_y = [System(*pair, py, my) for pair in COMPACT]
    beta = 4.0 * my * my
    sys_w = System(-beta, 1.0 + 2.0 * beta, {0: 1.0}, (0.0, 0.0), py, my)

    barrier = pltpu.get_barrier_semaphore()

    def greet(**device):
        pl.semaphore_signal(barrier, inc=1, device_id=device, device_id_type=MESH)

    for d in range(1, size):
        greet(gx=group * size + lax.rem(rank + d, size))
    for d in range(1, groups):
        greet(gx=lax.rem(group + d, groups) * size + rank)
    for d in range(1, py):
        greet(gy=lax.rem(wall + d, py))
    greet(gz=1 - core)
    is_last = (rank == size - 1) & (me < px - 1)
    is_first = (rank == 0) & (me > 0)

    @pl.when(is_last)
    def _():
        greet(gx=me + 1)

    @pl.when(is_first)
    def _():
        greet(gx=me - 1)

    reads = [pltpu.make_async_copy(v_hbm.at[c], v.at[c], load.at[c]) for c in range(nc)]
    reads.append(pltpu.make_async_copy(cp_hbm, cp, load.at[nc]))
    for read in reads:
        read.start()

    def remote(src, dst, send, recv, **target):
        return pltpu.make_async_remote_copy(
            src_ref=src, dst_ref=dst, send_sem=send, recv_sem=recv,
            device_id=target, device_id_type=MESH,
        )

    def arrived(ref, sem):
        pltpu.make_async_copy(ref, ref, sem).wait()

    def other(d, flip=False):
        if size & (size - 1):
            return lax.rem(rank + d, size)
        result, bit = 0, 1
        while bit < size:
            mine = lax.rem(rank // bit, 2)
            if bit == 1 and flip:
                mine = lax.rem(mine + core, 2)
            result = result + bit * ((1 - mine) if d & bit else mine)
            bit *= 2
        return result

    weigh_x = [
        [[pick(me, table[:, i]) for i in range(mx)] for table in (s.right, s.left)] for s in sys_x
    ]

    def sums_x(c):
        def step(b, _):
            part = [v[c, pl.ds(pl.multiple_of(i * my + b * 8, 8), 8), :] for i in range(mx)]
            for s in range(2):
                for way in range(2):
                    value = total([weigh_x[s][way][i] * part[i] for i in range(mx)])
                    flat = s * my + b * 8
                    owner = flat // rows
                    at = owner * 2 * rows + way * rows + lax.rem(flat, rows)
                    gx[c, pl.ds(pl.multiple_of(at, 8), 8), :] = value
            return 0

        lax.fori_loop(0, my // 8, step, 0)

    own = pl.ds(pl.multiple_of(rank * 2 * rows, 8), 2 * rows)
    for c in range(nc):
        reads[c].wait()
        sums_x(c)
        if c == 0:
            pl.semaphore_wait(
                barrier, size - 1 + groups - 1 + py - 1 + 1 + jnp.where(is_last | is_first, 1, 0)
            )
        for d in range(size - 1, 0, -1):
            t = other(d, d > 1)
            remote(
                gx.at[c, pl.ds(pl.multiple_of(t * 2 * rows, 8), 2 * rows)], gr.at[c, rank],
                sent.at[0], r1.at[c], gx=group * size + t,
            ).start()
        gr[c, rank] = gx[c, own, :]

    for c in range(nc):
        remote(v.at[c], zo.at[c], sent.at[1], zr.at[0], gz=1 - core).start()
    up = remote(v.at[:, pl.ds((mx - 1) * my, my)], xlo, hs.at[0], hr.at[0], gx=lax.rem(me + 1, px))
    down = remote(v.at[:, pl.ds(0, my)], xhi, hs.at[1], hr.at[1], gx=lax.rem(me + px - 1, px))

    @pl.when((me < px - 1) & (core == 0))
    def _():
        up.start()

    @pl.when((me > 0) & (core == 0))
    def _():
        down.start()

    def yrow(ref, c, y):
        return ref[c, pl.ds(y, mx, stride=my), :]

    weigh_y = [
        [[pick(wall, table[:, i]) for i in range(my)] for table in (s.right, s.left)] for s in sys_y
    ]

    def sums_y(c, _):
        sums = [[None, None], [None, None]]
        for i in range(my):
            row = yrow(v, c, i)
            vt[c, i] = row
            if i == 0:
                yout[c, 1, 0] = row
            if i == my - 1:
                yout[c, 0, 0] = row
            for s in range(2):
                for way in range(2):
                    term = weigh_y[s][way][i] * row
                    sums[s][way] = term if i == 0 else sums[s][way] + term
        for s in range(2):
            for way in range(2):
                yout[c, way, 1 + s] = sums[s][way]
        for d in range(1, py):
            peer = lax.rem(wall + d, py)
            way = jnp.where(peer > wall, 0, 1)
            remote(yout.at[c, way], yin.at[c, d - 1], sent.at[0], yr.at[0], gy=peer).start()
        return 0

    for c in range(nc):
        sums_y(c, 0)

    for i in range(my):
        shape_w[0, pl.ds(i, 1), :] = jnp.full((1, nz), sys_w.low[i], jnp.float32)
        shape_w[1, pl.ds(i, 1), :] = jnp.full((1, nz), sys_w.high[i], jnp.float32)

    slab = mx * my
    lane = lax.broadcasted_iota(jnp.int32, (slab, nz), 1)
    reads[nc].wait()

    def solve_z(c):
        def step(index, _):
            part = pl.ds(pl.multiple_of(index * slab, slab), slab)
            mine, rest = v[c, part, :], zo[c, part, :]

            def after(k):
                return pltpu.roll(jnp.where(lane < k, rest, mine), nz - k, 1)

            def before(k):
                return pltpu.roll(jnp.where(lane >= nz - k, rest, mine), k, 1)

            high, low = [after(k) for k in (1, 2, 3)], [before(k) for k in (1, 2, 3)]
            odd = [a - b for a, b in zip(high, low)]
            even = [a + b for a, b in zip(high, low)]
            first = (45.0 / 60.0) * odd[0] - (9.0 / 60.0) * odd[1] + (1.0 / 60.0) * odd[2]
            bend = (
                (viscosity * 2.0 / 180.0) * even[2] - (viscosity * 27.0 / 180.0) * even[1]
                + (viscosity * 270.0 / 180.0) * even[0] + (1.0 - viscosity * 490.0 / 180.0) * mine
            )
            conv[c, part, :] = v[2, part, :] * first
            expl[c, part, :] = bend - (time_step * zeta_old) * cp[c, part, :]
            return 0

        lax.fori_loop(0, mx * my // slab, step, 0)

    half = size // 2
    share = rank // half

    def table(field):
        return [
            pick(group * 2 + share, [field(sys_x[s], g * size + m) for g in range(groups) for s in range(2)])
            for m in range(size)
        ]

    t0, t1 = (table(lambda s, p, k=k: s.t[p, k]) for k in range(2))
    d0, d1, d2, d3 = (table(lambda s, p, k=k: s.d[p, k]) for k in range(4))

    def exchange(c):
        arrived(gr.at[c, pl.ds(0, size - 1)], r1.at[c])
        below, above = [None] * size, [None] * size
        for m in range(size):
            here = gr[c, m, pl.ds(0, rows), :]
            below[m] = here if m == 0 else here + t0[m] * below[m - 1]
        for m in reversed(range(size)):
            here = gr[c, m, pl.ds(rows, rows), :]
            above[m] = here if m == size - 1 else here + t1[m] * above[m + 1]
        if groups > 1:
            st[c, 0] = below[size - 1]
            st[c, 1] = above[0]
            for dg in range(1, groups):
                there = lax.rem(group + dg, groups)
                way = jnp.where(there > group, 0, 1)
                at = pl.multiple_of(4 * my + (dg - 1) * 2 * my + rank * rows, 8)
                for d in range(size - 1, -1, -1):
                    m = other(d, True)
                    remote(
                        st.at[c, way], ti.at[c, pl.ds(at, rows)], sent.at[0], r2.at[c],
                        gx=there * size + m,
                    ).start()
        for m in range(size):
            low = d1[m] * above[m]
            to[c, m, pl.ds(0, rows), :] = low if m == 0 else low + d0[m] * below[m - 1]
            high = d2[m] * below[m]
            to[c, m, pl.ds(rows, rows), :] = high if m == size - 1 else high + d3[m] * above[m + 1]
        for d in range(size - 1, 0, -1):
            t = other(d, d > 1)
            remote(to.at[c, t], ti.at[c, own], sent.at[0], r2.at[c], gx=group * size + t).start()
        ti[c, own, :] = to[c, rank]

    def gathered(system, side, by=1.0):
        def way(q, p):
            return 1 - side if q == p else (0 if q < p else 1)

        return [
            pick(wall, [by * system.weights[side, (p - d) % py, way((p - d) % py, p), p] for p in range(py)])
            for d in range(py)
        ]

    def side_of(systems, place, out):
        return [
            (
                pick(place, -out[s] * system.off * system.fix_low), pick(place, out[s] * system.edge_low),
                pick(place, -out[s] * system.off * system.fix_high), pick(place, out[s] * system.edge_high),
            )
            for s, system in enumerate(systems)
        ]

    near_y = side_of(sys_y, wall, OUT)
    outer_y = [[gathered(s, side, -OUT[k] * s.off) for side in range(2)] for k, s in enumerate(sys_y)]
    wide = WIDE

    def solve_y(index, _):
        c = index // (mx // wide)
        first_row = pl.multiple_of(lax.rem(index, mx // wide) * wide, wide)
        part = pl.ds(first_row, wide)
        cells = [jnp.where(wall > 0, yin[c, 0, 0, part, :], 0.0)]
        cells += [vt[c, y, part, :] for y in range(my)]
        cells += [jnp.where(wall < py - 1, yin[c, py - 2, 0, part, :], 0.0)]
        more = [
            [
                total(
                    [outer_y[s][side][0] * yout[c, 1 - side, 1 + s, part, :]]
                    + [outer_y[s][side][d] * yin[c, d - 1, 1 + s, part, :] for d in range(1, py)]
                    + [near_y[s][2 * side] * cells[0 - side], near_y[s][2 * side + 1] * cells[1 if side == 0 else my]]
                )
                for s in range(2)
            ]
            for side in range(2)
        ]
        for values, out in zip(line(sys_y, cells, *more), (fy, sy)):
            for i, value in enumerate(values):
                out[c, pl.ds(first_row * my + i, wide, stride=my), :] = value
        return 0

    near_x = side_of(sys_x, me, OUT)
    tile = 16 if my % 16 == 0 else 8

    def solve_x(index, _):
        c = index // (my // tile)
        start = pl.multiple_of(lax.rem(index, my // tile) * tile, tile)
        cells = [xlo[c, pl.ds(start, tile), :]]
        cells += [v[c, pl.ds(i * my + start, tile), :] for i in range(mx)]
        cells += [xhi[c, pl.ds(start, tile), :]]
        more = [
            [near_x[s][2 * side] * cells[0 - side] + near_x[s][2 * side + 1] * cells[1 if side == 0 else mx] for s in range(2)]
            for side in range(2)
        ]
        first, second = line(sys_x, cells, *more)
        for i in range(mx):
            part = pl.ds(i * my + start, tile)
            conv[c, part, :] = conv[c, part, :] + (v[0, part, :] * first[i] + v[1, part, :] * fy[c, part, :])
            expl[c, part, :] = expl[c, part, :] + (second[i] + sy[c, part, :])
        return 0

    for c in range(nc):
        exchange(c)

    @pl.when((me < px - 1) & (core == 1))
    def _():
        up.start()

    @pl.when((me > 0) & (core == 1))
    def _():
        down.start()

    arrived(zo, zr.at[0])
    for c in range(nc):
        solve_z(c)
    arrived(yin, yr.at[0])
    lax.fori_loop(0, nc * (mx // wide), solve_y, 0)

    @pl.when(me > 0)
    def _():
        up.wait_recv()

    @pl.when(me == 0)
    def _():
        xlo[...] = jnp.zeros_like(xlo)

    @pl.when(me < px - 1)
    def _():
        down.wait_recv()

    @pl.when(me == px - 1)
    def _():
        xhi[...] = jnp.zeros_like(xhi)

    lax.fori_loop(0, nc * (my // tile), solve_x, 0)

    def far(s, side, dg):
        values = []
        for p in range(px):
            g, q = p // size, (p // size - dg) % groups
            if q < g:
                value = s.d[p, 2 * side]
                for k in range((q + 1) * size, p + side):
                    value = value * s.t[k, 0]
            else:
                value = s.d[p, 2 * side + 1]
                for k in range(p + side, q * size):
                    value = value * s.t[k, 1]
            values.append(value)
        return pick(me, values)

    far_x = [[[far(s, side, dg) for dg in range(1, groups)] for side in range(2)] for s in sys_x]
    right_w = [pick(wall, sys_w.right[:, i]) for i in range(my)]
    left_w = [pick(wall, sys_w.left[:, i]) for i in range(my)]
    outer_w = [gathered(sys_w, side) for side in range(2)]
    back = 2 * rows * (size - 1) + (groups - 1) * 2 * my

    for c in range(nc):
        arrived(ti.at[c, pl.ds(0, back)], r2.at[c])
        outer = []
        for s in range(2):
            pair = []
            for side in range(2):
                value = jnp.concatenate(
                    [ti[c, pl.ds(b * 2 * rows + side * rows, rows), :] for b in range(s * half, (s + 1) * half)], axis=0
                )
                for dg in range(1, groups):
                    at = 4 * my + (dg - 1) * 2 * my + s * my
                    value = value + far_x[s][side][dg - 1] * ti[c, pl.ds(at, my), :]
                pair.append(value)
            outer.append(pair)
        for i in range(mx):
            part = pl.ds(i * my, my)
            more = sys_x[0].low[i] * outer[0][0] + sys_x[0].high[i] * outer[0][1]
            bend = (viscosity * sys_x[1].low[i]) * outer[1][0] + (viscosity * sys_x[1].high[i]) * outer[1][1]
            moved = conv[c, part, :] + v[0, part, :] * more
            conv[c, part, :] = moved
            expl[c, part, :] = expl[c, part, :] + (bend - (time_step * gamma_now) * moved)
        low = high = None
        for i in range(my):
            row = yrow(expl, c, i)
            et[c, i] = row
            low = right_w[i] * row if low is None else low + right_w[i] * row
            high = left_w[i] * row if high is None else high + left_w[i] * row
        gw[c, 0] = low
        gw[c, 1] = high
        for d in range(1, py):
            peer = lax.rem(wall + d, py)
            way = jnp.where(peer > wall, 0, 1)
            remote(gw.at[c, way], gwr.at[c, d - 1], sent.at[0], wr.at[0], gy=peer).start()

    def solve_w(c, _):
        for i, value in enumerate(sys_w.solve([et[c, y] for y in range(my)])):
            base[c, pl.ds(i, mx, stride=my), :] = value
        return 0

    lax.fori_loop(0, nc, solve_w, 0)
    arrived(gwr, wr.at[0])
    for c in range(nc):
        for side in range(2):
            ends_w[c, side] = total(
                [outer_w[side][0] * gw[c, 1 - side]]
                + [outer_w[side][d] * gwr[c, d - 1] for d in range(1, py)]
            )

    arrived(tally, sent.at[0])
    arrived(v, sent.at[1])

    @pl.when(me < px - 1)
    def _():
        up.wait_send()

    @pl.when(me > 0)
    def _():
        down.wait_send()


def finish(cfg, conv_in, base, ends_w, shape_w, conv, upd, built, sem):
    nc, mx, my = cfg
    writes = [pltpu.make_async_copy(conv_in.at[c], conv.at[c], sem.at[c]) for c in range(nc)]
    for write in writes:
        write.start()
    for c in range(nc):
        for i in range(mx):
            part = pl.ds(i * my, my)
            built[c, part, :] = base[c, part, :] + (
                shape_w[0] * ends_w[c, 0, pl.ds(i, 1), :] + shape_w[1] * ends_w[c, 1, pl.ds(i, 1), :]
            )
        write = pltpu.make_async_copy(built.at[c], upd.at[c], sem.at[nc + c])
        write.start()
        writes.append(write)
    for write in writes:
        write.wait()


def body(counts, velocity, conv_prev):
    px, py, pz = counts
    nc, mx, my, nz = velocity.shape
    size = 4 if px % 4 == 0 else 2
    groups = px // size
    rows = 2 * my // size
    assert pz == 2 and py > 1 and px % 2 == 0 and rows % 8 == 0 and mx % 8 == 0
    flat = (nc, mx * my, nz)
    f32 = jnp.float32
    sent = 2 * rows * (size - 1) * 2 + (groups - 1) * size * rows + (py - 1) * 4 * mx

    def vmem(*shape):
        return pltpu.VMEM(shape, f32)

    def dma(n):
        return pltpu.SemaphoreType.DMA((n,))

    def out(*shape):
        return jax.ShapeDtypeStruct(shape, f32)

    whole = pl.BlockSpec(memory_space=pltpu.VMEM)
    velocity = pltpu.with_memory_space_constraint(velocity.reshape(flat), pltpu.HBM)
    conv_prev = pltpu.with_memory_space_constraint(conv_prev.reshape(flat), pltpu.HBM)
    hbm = pl.BlockSpec(memory_space=pltpu.HBM)
    parts = pl.pallas_call(
        functools.partial(kernel, (nc, mx, my, nz, px, py, size, groups)),
        out_shape=[out(*flat), out(*flat), out(nc, 2, mx, nz), out(2, my, nz)],
        in_specs=[hbm, hbm],
        out_specs=[whole] * 4,
        scratch_shapes=[
            vmem(*flat), vmem(*flat), vmem(*flat),
            vmem(nc, my, nz), vmem(nc, my, nz),
            vmem(nc, 4 * my, nz), vmem(nc, size, 2 * rows, nz), vmem(nc, size, 2 * rows, nz),
            vmem(nc, 2, rows, nz), vmem(nc, 4 * my + (groups - 1) * 2 * my, nz),
            vmem(nc, 2, 3, mx, nz), vmem(nc, py - 1, 3, mx, nz),
            vmem(nc, my, mx, nz), vmem(*flat), vmem(*flat), vmem(*flat), vmem(nc, my, mx, nz),
            vmem(nc, 2, mx, nz), vmem(nc, py - 1, mx, nz), vmem(nc * sent, nz),
            dma(nc + 1), dma(nc), dma(nc), dma(1), dma(1), dma(1), dma(2), dma(2), dma(2),
        ],
        compiler_params=pltpu.CompilerParams(
            collective_id=0, has_side_effects=True, vmem_limit_bytes=32 * 1024 * 1024
        ),
    )(velocity, conv_prev)
    conv, upd = pl.pallas_call(
        functools.partial(finish, (nc, mx, my)),
        out_shape=[out(*flat), out(*flat)],
        in_specs=[whole] * 4,
        out_specs=[hbm, hbm],
        scratch_shapes=[vmem(*flat), dma(2 * nc)],
        compiler_params=pltpu.CompilerParams(vmem_limit_bytes=16 * 1024 * 1024),
    )(*parts)
    return conv.reshape(nc, mx, my, nz), upd.reshape(nc, mx, my, nz)


def solution(mesh):
    spec = P(None, "gx", "gy", "gz")
    counts = tuple(mesh.shape[name] for name in ("gx", "gy", "gz"))
    return jax.shard_map(
        functools.partial(body, counts), mesh=mesh, in_specs=(spec, spec),
        out_specs=(spec, spec), check_vma=False,
    )
```
